512 devices in a mesh: dp: 32 (over x, y, core), fsdp: 16 (over z).
Axes of the slice: x: 4, y: 4, z: 16, core: 2. Of those that a mesh axis runs over, the one named last changes fastest.
Arguments:
- query_pooled_states: bfloat16 [16, 512, 4096], P('fsdp', 'dp')
- passage_pooled_states: bfloat16 [16, 4096, 4096], P('fsdp', 'dp')
- query_attention_output: bfloat16 [16, 512, 4096], P('fsdp', 'dp'), may hold values from -0.059814453 to 0.059814453
- passage_attention_output: bfloat16 [16, 4096, 4096], P('fsdp', 'dp'), may hold values from -0.059814453 to 0.059814453
- positive_passage_row: int32 [16, 512], P('fsdp', 'dp'), may hold values from 0 to 127
- hard_negative_ids: int32 [16, 512, 64], P('fsdp', 'dp'), may hold values from 0 to 4095, as said below
- passage_home_row: int32 [16, 4096], P('fsdp'), may hold values from 0 to 4095, as said below
- adapter_down_weight: bfloat16 [16, 4096], P(None, 'fsdp'), may hold values from -0.09375 to 0.09375
- adapter_up_weight: bfloat16 [16, 4096], P(None, 'fsdp'), may hold values from -0.09375 to 0.09375
Outputs:
- grad_query_states: bfloat16 [16, 512, 4096], P('fsdp', 'dp')
- grad_passage_states: bfloat16 [16, 4096, 4096], P('fsdp', 'dp')
- adapter_down_gradient: float32 [16, 4096], P(None, 'fsdp')
- adapter_up_gradient: float32 [16, 4096], P(None, 'fsdp')
The draws below stay inside these ranges and needn't reach their ends.
Inputs may be any that keep to these rules, and one draw needn't show every extreme that they name: In each group the row is a permutation: passage p is row passage_home_row[g, p] of passage_pooled_states[g]. `hard_negative_ids`: ids of passages of the same group. The queries of one index of dp name at most 8 distinct passages held by any one index of dp, and in every group one index of dp holds exactly 8 distinct passages named by the queries of each index of dp. A query's list may repeat an id. `positive_passage_row`: the positive of query q is held by the query's own index of dp.
All inputs are finite; a program needn't handle non-finite values.
Results may differ from the reference program's by a relative error of at most 0.0062.
Values may be sent and summed in bfloat16 or wider, within the bound.
A program may use at most 64 MiB of HBM per device.

```python
import jax
import jax.numpy as jnp
from jax import lax

MODEL_WIDTH = 4096
ADAPTER_RANK = 16
NEG = 64
CAP = 8
Q_DEV = 16
P_DEV = 128
QUERIES = 512
PASSAGES = 4096
N_DP = 32
N_FSDP = 16


def layout_tables(key):
    home_keys = jax.random.split(jax.random.fold_in(key, 101), N_FSDP)
    home_rows = jax.vmap(lambda single: jax.random.permutation(single, PASSAGES))(home_keys).astype(jnp.int32)
    counts = jax.random.randint(jax.random.fold_in(key, 102), (N_FSDP, N_DP, N_DP), 1, CAP + 1)
    hottest = jax.random.randint(jax.random.fold_in(key, 103), (N_FSDP, 1, 1), 0, N_DP)
    counts = jnp.where(jnp.arange(N_DP)[None, None, :] == hottest, CAP, counts)
    keyed = jax.random.randint(jax.random.fold_in(key, 104), (N_FSDP, N_DP, N_DP, P_DEV), 0, 2 ** 20) * P_DEV + jnp.arange(P_DEV, dtype=jnp.int32)
    unused_top, chosen = lax.top_k(keyed, CAP)
    picked_rows = jnp.arange(N_DP, dtype=jnp.int32)[None, None, :, None] * P_DEV + chosen.astype(jnp.int32)
    usable = jnp.arange(CAP)[None, None, None, :] < counts[..., None]
    flat_width = N_DP * CAP
    picked_rows = picked_rows.reshape(N_FSDP, N_DP, flat_width)
    usable = usable.reshape(N_FSDP, N_DP, flat_width)
    ranks = jnp.cumsum(usable.astype(jnp.int32), axis=-1) - 1
    targets = jnp.where(usable, ranks, flat_width)
    group_ids = jnp.broadcast_to(jnp.arange(N_FSDP)[:, None, None], targets.shape)
    device_ids = jnp.broadcast_to(jnp.arange(N_DP)[None, :, None], targets.shape)
    pool_rows = jnp.zeros((N_FSDP, N_DP, flat_width), jnp.int32).at[group_ids, device_ids, targets].set(picked_rows, mode='drop')
    live_count = jnp.sum(usable.astype(jnp.int32), axis=-1)
    asks = Q_DEV * NEG
    picks = jax.random.randint(jax.random.fold_in(key, 105), (N_FSDP, N_DP, asks), 0, live_count[..., None])
    positions = jnp.arange(asks, dtype=jnp.int32)
    picks = jnp.where(positions[None, None, :] < live_count[..., None], positions[None, None, :], picks)
    shuffle_keys = jax.random.randint(jax.random.fold_in(key, 106), (N_FSDP, N_DP, asks), 0, 2 ** 16) * asks + positions
    ordering = jnp.argsort(shuffle_keys, axis=-1)
    picks = jnp.take_along_axis(picks, ordering, axis=-1)
    wanted_rows = jnp.take_along_axis(pool_rows, picks, axis=-1)
    inverse_home = jnp.argsort(home_rows, axis=-1).astype(jnp.int32)
    passage_ids = jnp.take_along_axis(inverse_home, wanted_rows.reshape(N_FSDP, N_DP * asks), axis=1)
    return (home_rows, passage_ids.reshape(N_FSDP, QUERIES, NEG).astype(jnp.int32))


def passage_base(key):
    return jax.random.normal(jax.random.fold_in(key, 204), (N_FSDP, PASSAGES, MODEL_WIDTH))


def draw_passage_home_row(key, part):
    return layout_tables(key)[0]


def draw_hard_negative_ids(key, part):
    return layout_tables(key)[1]


def draw_passage_pooled_states(key, part):
    return passage_base(key).astype(jnp.bfloat16)


def draw_query_pooled_states(key, part):
    return jax.random.normal(jax.random.fold_in(key, 213), (N_FSDP, QUERIES, MODEL_WIDTH)).astype(jnp.bfloat16)


def with_ends(drawn, key, smallest, largest):
    longest = drawn.shape.index(max(drawn.shape))
    spots = []
    for shift in (0, 1):
        where = [jax.random.randint(jax.random.fold_in(key, axis), (), 0, length) for axis, length in enumerate(drawn.shape)]
        where[longest] = (where[longest] + shift) % drawn.shape[longest]
        spots.append(tuple(where))
    return drawn.at[spots[0]].set(smallest).at[spots[1]].set(largest)


def raised(drawn, key, source, target, blocks, factor):
    def block_of(axis_at):
        return (jnp.arange(drawn.shape[axis_at]) // (drawn.shape[axis_at] // blocks)).reshape((-1,) + (1,) * (drawn.ndim - 1 - axis_at))

    first = jax.random.permutation(key, blocks)[block_of(target)]
    second = (block_of(target) + blocks // 2) % blocks
    return jnp.where((block_of(source) == first) | (block_of(source) == second), factor * drawn, drawn)


def shard_levels(stream_key, extent, shards, low, top_value):
    def one(dim, parts):
        draws = jax.random.uniform(jax.random.fold_in(jax.random.fold_in(stream_key, 6), dim), (parts,), jnp.float32, low / len(shards), top_value / len(shards))
        return jnp.repeat(jnp.exp(draws), extent[dim] // parts).reshape((-1,) + (1,) * (len(extent) - dim - 1))

    level = one(*shards[0])
    for cut in shards[1:]:
        level = level * one(*cut)
    return level


def centred(stream_key, shape, spread, reach, shards=(), held_as=jnp.bfloat16):
    loudness = shard_levels(stream_key, shape, shards, -0.22, 0.18) if shards else 1.0
    array = jax.random.normal(stream_key, shape, jnp.float32) * spread * loudness
    return jnp.minimum(jnp.maximum(array, -reach), reach).astype(held_as)


def heavy_noise(rng, extent, deviation, limit, cuts, heavy, kind=jnp.bfloat16):
    array = deviation * jax.random.normal(rng, extent, jnp.float32)
    if cuts:
        array = array * shard_levels(rng, extent, cuts, -0.22, 0.18)
    return jnp.clip(raised(array, jax.random.fold_in(rng, 3), *heavy), -limit, limit).astype(kind)


def setup_inputs(seed: int = 0) -> dict:
    splits = jax.random.split(jax.random.key(seed), 10)
    query_pooled_states = draw_query_pooled_states(jax.random.fold_in(splits[9], 71), 0)
    passage_pooled_states = draw_passage_pooled_states(jax.random.fold_in(splits[9], 71), 0)
    query_attention_output = heavy_noise(splits[2], (N_FSDP, QUERIES, MODEL_WIDTH), 0.01, 0.059814453, ((0, 16), (1, 32)), (0, 2, 16, 2.0))
    passage_attention_output = heavy_noise(splits[3], (N_FSDP, PASSAGES, MODEL_WIDTH), 0.01, 0.059814453, ((0, 16), (1, 32)), (0, 2, 16, 2.0))
    positive_passage_row = with_ends(jax.random.randint(splits[4], (N_FSDP, QUERIES), 0, P_DEV), jax.random.fold_in(splits[4], 1), 0, P_DEV - 1).astype(jnp.int32)
    hard_negative_ids = draw_hard_negative_ids(jax.random.fold_in(splits[9], 71), 0)
    passage_home_row = draw_passage_home_row(jax.random.fold_in(splits[9], 71), 0)
    adapter_down_weight = centred(splits[7], (ADAPTER_RANK, MODEL_WIDTH), MODEL_WIDTH ** -0.5, 0.09375, ((1, 16),))
    adapter_up_weight = centred(splits[8], (ADAPTER_RANK, MODEL_WIDTH), MODEL_WIDTH ** -0.5, 0.09375, ((1, 16),))
    return dict(query_pooled_states=query_pooled_states, passage_pooled_states=passage_pooled_states, query_attention_output=query_attention_output, passage_attention_output=passage_attention_output, positive_passage_row=positive_passage_row, hard_negative_ids=hard_negative_ids, passage_home_row=passage_home_row, adapter_down_weight=adapter_down_weight, adapter_up_weight=adapter_up_weight)


SOFTMAX_HEAT = 0.01
ADAPTER_SCALE = 2.0
EPSILON = 1e-06

def unit_rows(raw_rows):
    values = raw_rows.astype(jnp.float32)
    lengths = jnp.sqrt(lax.optimization_barrier(jnp.sum(values * values, axis=-1, keepdims=True)) + EPSILON)
    return (values / lengths, lengths)

def norm_backward(unit_vec, lengths, upstream):
    inner_sum = lax.optimization_barrier(jnp.sum(unit_vec * upstream, axis=-1, keepdims=True))
    return ((upstream - unit_vec * inner_sum) / lengths).astype(jnp.bfloat16)

def reference(query_pooled_states, passage_pooled_states, query_attention_output, passage_attention_output, positive_passage_row, hard_negative_ids, passage_home_row, adapter_down_weight, adapter_up_weight):

    def one_group(inputs):
        query_raw, passage_raw, query_input_rows, passage_input_rows, positives, negatives, home_rows = inputs
        query_unit, query_length = unit_rows(query_raw)
        passage_unit, passage_length = unit_rows(passage_raw)
        query_vectors = query_unit.astype(jnp.bfloat16)
        passage_vectors = passage_unit.astype(jnp.bfloat16)
        query_index = jnp.arange(QUERIES, dtype=jnp.int32)
        positive_row = (query_index // Q_DEV * P_DEV + positives).astype(jnp.int32)
        negative_rows = home_rows[negatives].astype(jnp.int32)
        candidates = jnp.concatenate([positive_row[:, None], negative_rows], axis=1)
        score_matrix = jnp.dot(query_vectors, passage_vectors.T, preferred_element_type=jnp.float32) / SOFTMAX_HEAT
        scores = jnp.take_along_axis(score_matrix, candidates, axis=1)
        softmax_probabilities = jax.nn.softmax(scores, axis=-1)
        target_index = (jnp.arange(NEG + 1) == 0).astype(jnp.float32)
        score_gradient = (softmax_probabilities - target_index[None, :]) / SOFTMAX_HEAT
        pair_weight = jnp.zeros((QUERIES, PASSAGES), jnp.float32).at[query_index[:, None], candidates].add(score_gradient)
        query_upstream = jnp.dot(pair_weight, passage_vectors.astype(jnp.float32), precision=lax.Precision.HIGHEST)
        passage_upstream = jnp.dot(pair_weight.T, query_vectors.astype(jnp.float32), precision=lax.Precision.HIGHEST)
        query_gradient = norm_backward(query_unit, query_length, query_upstream)
        passage_gradient = norm_backward(passage_unit, passage_length, passage_upstream)
        input_stack = jnp.concatenate([query_input_rows, passage_input_rows], axis=0)
        gradient_stack = jnp.concatenate([query_gradient, passage_gradient], axis=0)
        rank_projection = jnp.dot(input_stack, adapter_down_weight.T, preferred_element_type=jnp.float32).astype(jnp.bfloat16)
        up_sum = jnp.dot(rank_projection.T, gradient_stack, preferred_element_type=jnp.float32)
        rank_gradient = jnp.dot(gradient_stack, adapter_up_weight.T, preferred_element_type=jnp.float32).astype(jnp.bfloat16)
        down_sum = jnp.dot(rank_gradient.T, input_stack, preferred_element_type=jnp.float32)
        return (query_gradient, passage_gradient, down_sum, up_sum)
    output_tuple = lax.map(one_group, (query_pooled_states, passage_pooled_states, query_attention_output, passage_attention_output, positive_passage_row, hard_negative_ids, passage_home_row))
    adapter_down_gradient = ADAPTER_SCALE * lax.optimization_barrier(jnp.sum(output_tuple[2], axis=0))
    adapter_up_gradient = ADAPTER_SCALE * lax.optimization_barrier(jnp.sum(output_tuple[3], axis=0))
    return (output_tuple[0], output_tuple[1], adapter_down_gradient, adapter_up_gradient)
```

```python
import jax
import jax.numpy as jnp
from jax import lax
from jax.experimental import pallas as pl
from jax.experimental.pallas import tpu as pltpu
from jax.sharding import PartitionSpec as P

MESH = pl.DeviceIdType.MESH
F32, BF16, I32 = jnp.float32, jnp.bfloat16, jnp.int32
HEAT = 100.0
ADAPTER_SCALE = 2.0
EPSILON = 1e-06
D = 4096
H = 2048
T = 512
NN = (((1,), (0,)), ((), ()))
NT = (((1,), (1,)), ((), ()))


def dot(lhs, rhs, dims=NN):
    return lax.dot_general(lhs, rhs, dims, preferred_element_type=F32)


def hi_lo(w):
    hi = w.astype(BF16)
    return hi, (w - hi.astype(F32)).astype(BF16)


def lanes_sum(v):
    return jnp.sum(v, axis=-1, keepdims=True)


def kernel(
    q_ref, p_ref, aq_ref, ap_ref, neg_ref, pos_ref, home_ref, aw_ref, bw_ref,
    gq_ref, gp_ref, res_ref,
    qown, qoth, pb, ab, negp, lhs, rhs, cnt, ssnd, srcv, wsnd, wown, woth,
    t1, rl1, d1p, d1m, r1m, r1p, uf, v1, t2, rl2, d2p, d2m, r2m, r2p,
    pup, dsum, dbuf, drow, rrow, zrow, zbuf, orow, oall,
    ag_s, q_r, qo_r, p_s, p_r, ab_s, ab_r, s_s, s_r, w_s, w_r, wo_s, wo_r,
    rs_s, rs_r, d_s, d_r, rr_s, rr_r, z_s, z_r, o_s, o_r,
):
    dp, z = lax.axis_index("dp"), lax.axis_index("fsdp")
    core, chip = lax.rem(dp, 2), dp // 2
    x, y = chip // 4, lax.rem(chip, 4)
    a = x * (1 - core) + y * core
    b = y * (1 - core) + x * core
    sa, sb = 8 - 6 * core, 2 + 6 * core
    other = 1 - core

    def near(v, k):
        return lax.rem(v + k, 4)

    def at(a_, b_):
        return (a_ * sa + b_ * sb + core, z)

    def slot(a_, b_):
        return b_ * 4 + a_

    me = slot(a, b)
    partner = (chip * 2 + other, z)
    am, a2, ap = near(a, 3), near(a, 2), near(a, 1)
    bm, b2, bp = near(b, 3), near(b, 2), near(b, 1)

    barrier = pltpu.get_barrier_semaphore()

    @pl.loop(1, 32)
    def _(k):
        pl.semaphore_signal(barrier, inc=1, device_id=(lax.rem(dp + k, 32), z), device_id_type=MESH)

    @pl.loop(1, 16)
    def _(k):
        pl.semaphore_signal(barrier, inc=1, device_id=(dp, lax.rem(z + k, 16)), device_id_type=MESH)

    qv = q_ref[...].astype(F32)
    q_len = jnp.sqrt(lanes_sum(qv * qv) + EPSILON)
    qe = (qv * (1.0 / q_len)).astype(BF16)
    qown[me, 0] = qe[:, :H]
    qown[me, 1] = qe[:, H:]

    def p_rows(i, carry):
        rows = pl.ds(pl.multiple_of(i * 32, 32), 32)
        pv = p_ref[rows, :].astype(F32)
        p_len = jnp.sqrt(lanes_sum(pv * pv) + EPSILON)
        dst = pl.ds(pl.multiple_of(core * 128 + i * 32, 32), 32)
        pb[dst, :] = (pv * (1.0 / p_len)).astype(BF16)
        return carry

    lax.fori_loop(0, 4, p_rows, 0)
    zcols = pl.ds(pl.multiple_of(z * 256, 256), 256)
    ab[0:16, zcols] = aw_ref[...]
    ab[16:32, zcols] = bw_ref[...]

    pl.semaphore_wait(barrier, 46)

    sent = []

    def push(src, dst, ssem, rsem, device):
        c = pltpu.make_async_remote_copy(
            src_ref=src, dst_ref=dst, send_sem=ssem, recv_sem=rsem, device_id=device, device_id_type=MESH
        )
        c.start()
        return c

    def arrive(dst, rsem, ssem):
        pltpu.make_async_remote_copy(
            src_ref=dst, dst_ref=dst, send_sem=ssem, recv_sem=rsem, device_id=partner, device_id_type=MESH
        ).wait_recv()

    def gone(src, ssem, rsem):
        pltpu.make_async_remote_copy(
            src_ref=src, dst_ref=src, send_sem=ssem, recv_sem=rsem, device_id=partner, device_id_type=MESH
        ).wait_send()

    def q_full(s, device):
        n = len(sent)
        sent.append(push(qown.at[s], qown.at[s], ag_s.at[n], q_r.at[s, 0], device))

    def q_half(s, h, device):
        n = len(sent)
        sent.append(push(qown.at[s, h], qown.at[s, h], ag_s.at[n], q_r.at[s, h], device))

    def q_other(s):
        n = len(sent)
        sent.append(push(qown.at[s], qoth.at[s], ag_s.at[n], qo_r.at[s], partner))

    def got_full(s):
        arrive(qown.at[s], q_r.at[s, 0], ag_s.at[0])

    def got_halves(s):
        arrive(qown.at[s, 0], q_r.at[s, 0], ag_s.at[0])
        arrive(qown.at[s, 1], q_r.at[s, 1], ag_s.at[0])

    q_full(me, at(ap, b))
    q_full(me, at(am, b))
    q_full(me, at(a, bp))
    q_full(me, at(a, bm))
    own_rows = pl.ds(pl.multiple_of(core * 128, 128), 128)
    other_rows = pl.ds(pl.multiple_of(other * 128, 128), 128)
    p_copy = push(pb.at[own_rows], pb.at[own_rows], p_s, p_r, partner)
    q_other(me)

    @pl.loop(1, 16)
    def _(k):
        push(ab.at[:, zcols], ab.at[:, zcols], ab_s.at[k], ab_r.at[z], (dp, lax.rem(z + k, 16)))

    negp[...] = jnp.full((16, 128), -1, I32)
    negp[:, 0:64] = neg_ref[...]
    n_row = jnp.concatenate([negp[k : k + 1, :] for k in range(16)], axis=1)
    home = home_ref[...]
    table = jnp.concatenate(
        [(home >> 7).astype(F32).T, (home & 127).astype(F32).T], axis=0
    ).astype(BF16)
    for part in range(4):
        n = n_row[:, part * T : (part + 1) * T]
        lane_q = (lax.broadcasted_iota(I32, (1, T), 1) >> 7) + part * 4
        picked = (lax.broadcasted_iota(I32, (32, T), 0) == (n >> 7)).astype(F32).astype(BF16)
        found = dot(table, picked)
        low = lax.broadcasted_iota(I32, (128, T), 0) == (n & 127)
        dev_row = jnp.sum(jnp.where(low, found[0:128], 0.0), axis=0, keepdims=True).astype(I32)
        in_dev = jnp.sum(jnp.where(low, found[128:256], 0.0), axis=0, keepdims=True).astype(I32)
        chip_row = dev_row >> 1
        key = ((chip_row >> 2) * (1 + 3 * core) + (chip_row & 3) * (4 - 3 * core)) * 16 + lane_q
        key = jnp.where(n >= 0, key, -1)
        col = (dev_row & 1) * 128 + in_dev
        rows = lax.broadcasted_iota(I32, (256, T), 0)
        lhs[:, part * T : (part + 1) * T] = (rows == key).astype(F32).astype(BF16)
        rhs[:, part * T : (part + 1) * T] = (rows == col).astype(F32).astype(BF16)
    times = dot(lhs[...], rhs[...], NT)
    cnt[:, 0] = times[:, 0:128].reshape(16, 16, 128)
    cnt[:, 1] = times[:, 128:256].reshape(16, 16, 128)
    pos = jnp.zeros((16, 128), I32)
    for k in range(16):
        pos = jnp.where(lax.broadcasted_iota(I32, (16, 128), 0) == k, pos_ref[0, k], pos)
    is_pos = (lax.broadcasted_iota(I32, (16, 128), 1) == pos).astype(F32)
    cnt[me, core] = cnt[me, core] + is_pos

    def scores(b_):
        block = pl.ds(b_ * 4, 4)
        s = dot(qown[block, 0].reshape(64, H), pb[:, 0:H], NT)
        s = (s + dot(qown[block, 1].reshape(64, H), pb[:, H:D], NT)) * HEAT
        ssnd[block, 0] = s[:, 0:128].reshape(4, 16, 128)
        ssnd[block, 1] = s[:, 128:256].reshape(4, 16, 128)

    def send_scores(b_, skip_own):
        for i in range(4):
            if skip_own and i == 0:
                continue
            a_ = near(a, i)
            s = slot(a_, b_)
            push(ssnd.at[s], srcv.at[me], s_s.at[s], s_r.at[me], at(a_, b_))

    got_full(slot(am, b))
    q_half(slot(am, b), 0, at(ap, b))
    q_full(slot(am, b), at(a, bp))
    q_full(slot(am, b), at(a, bm))
    got_full(slot(ap, b))
    q_half(slot(ap, b), 1, at(am, b))
    q_full(slot(ap, b), at(a, bp))
    q_full(slot(ap, b), at(a, bm))
    q_other(slot(am, b))
    q_other(slot(ap, b))
    got_full(slot(a, bm))
    q_half(slot(a, bm), 0, at(a, bp))
    got_full(slot(a, bp))
    q_half(slot(a, bp), 1, at(a, bm))
    got_halves(slot(a2, b))
    q_full(slot(a2, b), at(a, bp))
    q_full(slot(a2, b), at(a, bm))
    q_other(slot(a2, b))
    q_other(slot(a, bm))
    q_other(slot(a, bp))
    arrive(pb.at[other_rows], p_r, p_s)
    scores(b)
    send_scores(b, True)
    srcv[me] = ssnd[me]
    for a_ in (am, ap, a2):
        got_full(slot(a_, bm))
        q_half(slot(a_, bm), 0, at(a, bp))
        got_full(slot(a_, bp))
        q_half(slot(a_, bp), 1, at(a, bm))
        q_other(slot(a_, bm))
        q_other(slot(a_, bp))
    scores(bm)
    send_scores(bm, False)
    scores(bp)
    send_scores(bp, False)
    for a_ in (a, am, ap, a2):
        got_halves(slot(a_, b2))
    scores(b2)
    send_scores(b2, False)
    for a_ in (a, am, ap, a2):
        q_other(slot(a_, b2))

    @pl.loop(1, 16)
    def _(k):
        zk = lax.rem(z + k, 16)
        cols = pl.ds(pl.multiple_of(zk * 256, 256), 256)
        arrive(ab.at[:, cols], ab_r.at[zk], ab_s.at[1])

    low_p = dot(ab[0:16, :], ap_ref[...], NT).astype(BF16)
    low_q = dot(ab[0:16, :], aq_ref[...], NT).astype(BF16)

    def peers(body):
        @pl.loop(1, 16)
        def _(k):
            a_, b_ = near(a, lax.rem(k, 4)), near(b, k // 4)
            body(a_, b_, slot(a_, b_))

    peers(lambda a_, b_, s: arrive(srcv.at[s], s_r.at[s], s_s.at[0]))

    low_value = jnp.full((16, 128), -1e30, F32)

    def top_of(s, m):
        m = jnp.maximum(m, jnp.where(cnt[s, 0] > 0.0, srcv[s, 0], low_value))
        return jnp.maximum(m, jnp.where(cnt[s, 1] > 0.0, srcv[s, 1], low_value))

    top = low_value
    for s in range(16):
        top = top_of(s, top)
    top = jnp.max(top, axis=-1, keepdims=True)
    total = jnp.zeros((16, 128), F32)
    for s in range(16):
        for k in range(2):
            c = cnt[s, k]
            e = c * jnp.exp(jnp.where(c > 0.0, srcv[s, k] - top, low_value))
            wsnd[s, k] = e
            total = total + e
    scale = HEAT / lanes_sum(total)
    for s in range(16):
        for k in range(2):
            wsnd[s, k] = wsnd[s, k] * scale
    wsnd[me, core] = wsnd[me, core] - HEAT * is_pos

    peers(lambda a_, b_, s: push(wsnd.at[s], wown.at[me], w_s.at[s], w_r.at[me], at(a_, b_)))

    @pl.loop(0, 16)
    def _(k):
        a_, b_ = near(a, lax.rem(k, 4)), near(b, k // 4)
        s = slot(a_, b_)
        push(wsnd.at[s, other], woth.at[me], wo_s.at[s], wo_r.at[me], (a_ * sa + b_ * sb + other, z))

    wown[me] = wsnd[me]
    peers(lambda a_, b_, s: arrive(wown.at[s], w_r.at[s], w_s.at[0]))

    def shares(b_, h, put):
        block = pl.ds(b_ * 4, 4)
        w = jnp.concatenate([wown[block, 0].reshape(64, 128), wown[block, 1].reshape(64, 128)], axis=1)
        w = jnp.concatenate(hi_lo(w), axis=0)
        for j in range(H // T):
            r = dot(w, pb[:, h * H + j * T : h * H + (j + 1) * T])
            put(slice(j * T, (j + 1) * T), (r[0:64] + r[64:128]).reshape(4, 16, T))

    def put_in(ref, *where):
        def put(cols, r):
            ref[(*where, slice(None), slice(None), cols)] = r.astype(ref.dtype)

        return put

    rs = []

    def hop(src, dst, device):
        n = len(rs)
        rs.append(push(src, dst, rs_s.at[n], rs_r.at[n], device))

    def landed(dst, n):
        arrive(dst, rs_r.at[n], rs_s.at[0])

    shares(b2, 0, put_in(t1, 0))
    hop(t1.at[0], rl1.at[0], at(a, bp))
    shares(b2, 1, put_in(t1, 1))
    hop(t1.at[1], rl1.at[1], at(a, bm))
    shares(bp, 1, put_in(d1p, 1))
    hop(d1p.at[1], r1m.at[1], at(a, bp))
    shares(bm, 0, put_in(d1m, 0))
    hop(d1m.at[0], r1p.at[0], at(a, bm))
    shares(bp, 0, put_in(uf, 0))
    shares(bm, 1, put_in(uf, 1))
    landed(rl1.at[0], 0)
    d1p[0] = (uf[0] + rl1[0].astype(F32)).astype(BF16)
    hop(d1p.at[0], r1m.at[0], at(a, bp))
    landed(rl1.at[1], 1)
    d1m[1] = (uf[1] + rl1[1].astype(F32)).astype(BF16)
    hop(d1m.at[1], r1p.at[1], at(a, bm))
    shares(b, 0, put_in(v1, 0))
    shares(b, 1, put_in(v1, 1))

    for a_, b_ in ((am, b), (ap, b), (a2, b), (a, bm), (a, bp), (a, b)):
        arrive(qoth.at[slot(a_, b_)], qo_r.at[slot(a_, b_)], ag_s.at[0])
    for a_ in (am, ap, a2):
        for b_ in (bm, bp):
            arrive(qoth.at[slot(a_, b_)], qo_r.at[slot(a_, b_)], ag_s.at[0])
    for a_ in (a, am, ap, a2):
        arrive(qoth.at[slot(a_, b2)], qo_r.at[slot(a_, b2)], ag_s.at[0])

    @pl.loop(0, 16)
    def _(s):
        arrive(woth.at[s], wo_r.at[s], wo_s.at[0])

    wt = jnp.concatenate([wown[:, core].reshape(256, 128).T, woth[...].reshape(256, 128).T], axis=1)
    wt = jnp.concatenate(hi_lo(wt), axis=0)
    p_sq = jnp.zeros((128, 1), F32)
    p_in = jnp.zeros((128, 1), F32)
    for h in range(2):
        for j in range(H // T):
            cols = slice(h * H + j * T, h * H + (j + 1) * T)
            sub = slice(j * T, (j + 1) * T)
            r = dot(wt[:, 0:256], qown[:, h, :, sub].reshape(256, T))
            r = r + dot(wt[:, 256:512], qoth[:, h, :, sub].reshape(256, T))
            r = r[0:128] + r[128:256]
            pv = p_ref[:, cols].astype(F32)
            p_sq = p_sq + lanes_sum(pv * pv)
            p_in = p_in + lanes_sum(pv * r)
            pup[:, cols] = r
    p_inv = 1.0 / jnp.sqrt(p_sq + EPSILON)
    p_in = p_in * p_inv * p_inv
    for j in range(D // T):
        cols = slice(j * T, (j + 1) * T)
        gp_ref[:, cols] = ((pup[:, cols] - p_ref[:, cols].astype(F32) * p_in) * p_inv).astype(BF16)

    landed(r1m.at[1], 2)
    landed(r1p.at[0], 3)
    landed(r1m.at[0], 4)
    landed(r1p.at[1], 5)
    for h in range(2):
        v1[h] = v1[h] + r1m[h].astype(F32) + r1p[h].astype(F32)
        t2[h] = v1[h, a2].astype(BF16)
        if h == 0:
            hop(t2.at[0], rl2.at[0], at(ap, b))
            d2m[0] = v1[0, am].astype(BF16)
            hop(d2m.at[0], r2p.at[0], at(am, b))
        else:
            hop(t2.at[1], rl2.at[1], at(am, b))
            d2p[1] = v1[1, ap].astype(BF16)
            hop(d2p.at[1], r2m.at[1], at(ap, b))
    landed(rl2.at[0], 6)
    d2p[0] = (v1[0, ap] + rl2[0].astype(F32)).astype(BF16)
    hop(d2p.at[0], r2m.at[0], at(ap, b))
    landed(rl2.at[1], 8)
    d2m[1] = (v1[1, am] + rl2[1].astype(F32)).astype(BF16)
    hop(d2m.at[1], r2p.at[1], at(am, b))

    back_p = dot(ab[16:32, :], gp_ref[...], NT).astype(BF16)
    for j in range(D // T):
        cols = slice(j * T, (j + 1) * T)
        dsum[0:16, cols] = dot(back_p, ap_ref[:, cols])
        dsum[16:32, cols] = dot(low_p, gp_ref[:, cols])

    landed(r2p.at[0], 7)
    landed(r2m.at[1], 9)
    landed(r2m.at[0], 10)
    landed(r2p.at[1], 11)
    qu = jnp.concatenate(
        [v1[h, a] + r2m[h].astype(F32) + r2p[h].astype(F32) for h in range(2)], axis=1
    )
    qv = q_ref[...].astype(F32)
    q_inv = 1.0 / jnp.sqrt(lanes_sum(qv * qv) + EPSILON)
    q_in = lanes_sum(qv * qu) * q_inv * q_inv
    gq = ((qu - qv * q_in) * q_inv).astype(BF16)
    gq_ref[...] = gq
    back_q = dot(ab[16:32, :], gq, NT).astype(BF16)
    for j in range(D // T):
        cols = slice(j * T, (j + 1) * T)
        dsum[0:16, cols] = ADAPTER_SCALE * (dsum[0:16, cols] + dot(back_q, aq_ref[:, cols]))
        dsum[16:32, cols] = ADAPTER_SCALE * (dsum[16:32, cols] + dot(low_q, gq[:, cols]))

    mine = pl.ds(pl.multiple_of(core * 16, 16), 16)
    theirs = pl.ds(pl.multiple_of(other * 16, 16), 16)
    d_copy = push(dsum.at[theirs], dbuf, d_s, d_r, partner)
    arrive(dbuf, d_r, d_s)
    for j in range(D // 128):
        cols = slice(j * 128, (j + 1) * 128)
        drow[:, j // 2, j % 2, :] = dsum[mine, cols] + dbuf[:, cols]
    peers(lambda a_, b_, s: push(drow.at[s], rrow.at[me], rr_s.at[s], rr_r.at[me], at(a_, b_)))
    rrow[me] = drow[me]
    peers(lambda a_, b_, s: arrive(rrow.at[s], rr_r.at[s], rr_s.at[0]))
    acc = rrow[0]
    for s in range(1, 16):
        acc = acc + rrow[s]
    zrow[...] = acc

    @pl.loop(1, 16)
    def _(k):
        zk = lax.rem(z + k, 16)
        push(zrow.at[zk], zbuf.at[z], z_s.at[zk], z_r.at[z], (dp, zk))

    zbuf[z] = zrow[z]

    @pl.loop(1, 16)
    def _(k):
        zk = lax.rem(z + k, 16)
        arrive(zbuf.at[zk], z_r.at[zk], z_s.at[0])

    acc = zbuf[0]
    for s in range(1, 16):
        acc = acc + zbuf[s]
    orow[...] = acc
    oall[core, me] = acc

    @pl.loop(1, 32)
    def _(k):
        push(orow, oall.at[core, me], o_s.at[k], o_r.at[core, me], (lax.rem(dp + k, 32), z))

    @pl.loop(1, 32)
    def _(k):
        d_ = lax.rem(dp + k, 32)
        c_, h_ = lax.rem(d_, 2), d_ // 2
        s_ = (h_ // 4) * (1 + 3 * c_) + lax.rem(h_, 4) * (4 - 3 * c_)
        arrive(oall.at[c_, s_], o_r.at[c_, s_], o_s.at[1])

    res_ref[...] = oall[...]

    for c in sent + rs + [p_copy, d_copy]:
        c.wait_send()

    @pl.loop(1, 16)
    def _(k):
        a_, b_ = near(a, lax.rem(k, 4)), near(b, k // 4)
        s = slot(a_, b_)
        gone(ssnd.at[s], s_s.at[s], s_r.at[s])
        gone(wsnd.at[s], w_s.at[s], w_r.at[s])
        gone(drow.at[s], rr_s.at[s], rr_r.at[s])
        zk = lax.rem(z + k, 16)
        gone(zrow.at[zk], z_s.at[zk], z_r.at[zk])
        gone(ab.at[:, zcols], ab_s.at[k], ab_r.at[z])

    @pl.loop(0, 16)
    def _(k):
        gone(wsnd.at[k, other], wo_s.at[k], wo_r.at[k])

    @pl.loop(1, 32)
    def _(k):
        gone(orow, o_s.at[k], o_r.at[0, 0])


VM = pl.BlockSpec(memory_space=pltpu.VMEM)
SM = pl.BlockSpec(memory_space=pltpu.SMEM)


def per_device(query, passage, query_attn, passage_attn, positives, negatives, home, down, up):
    block = (16, 2, 16, 128)
    dma = pltpu.SemaphoreType.DMA
    grad_q, grad_p, res = pl.pallas_call(
        kernel,
        out_shape=(
            jax.ShapeDtypeStruct((16, D), BF16),
            jax.ShapeDtypeStruct((128, D), BF16),
            jax.ShapeDtypeStruct((2, 16, 2, 128), F32),
        ),
        in_specs=[VM, VM, VM, VM, VM, SM, VM, VM, VM],
        out_specs=(VM, VM, VM),
        scratch_shapes=[
            pltpu.VMEM((16, 2, 16, H), BF16),
            pltpu.VMEM((16, 2, 16, H), BF16),
            pltpu.VMEM((256, D), BF16),
            pltpu.VMEM((32, D), BF16),
            pltpu.VMEM((16, 128), I32),
            pltpu.VMEM((256, H), BF16),
            pltpu.VMEM((256, H), BF16),
            pltpu.VMEM(block, F32),
            pltpu.VMEM(block, F32),
            pltpu.VMEM(block, F32),
            pltpu.VMEM(block, F32),
            pltpu.VMEM(block, F32),
            pltpu.VMEM((16, 16, 128), F32),
            pltpu.VMEM((2, 4, 16, H), BF16),
            pltpu.VMEM((2, 4, 16, H), BF16),
            pltpu.VMEM((2, 4, 16, H), BF16),
            pltpu.VMEM((2, 4, 16, H), BF16),
            pltpu.VMEM((2, 4, 16, H), BF16),
            pltpu.VMEM((2, 4, 16, H), BF16),
            pltpu.VMEM((2, 4, 16, H), F32),
            pltpu.VMEM((2, 4, 16, H), F32),
            pltpu.VMEM((2, 16, H), BF16),
            pltpu.VMEM((2, 16, H), BF16),
            pltpu.VMEM((2, 16, H), BF16),
            pltpu.VMEM((2, 16, H), BF16),
            pltpu.VMEM((2, 16, H), BF16),
            pltpu.VMEM((2, 16, H), BF16),
            pltpu.VMEM((128, D), F32),
            pltpu.VMEM((32, D), F32),
            pltpu.VMEM((16, D), F32),
            pltpu.VMEM((16, 16, 2, 128), F32),
            pltpu.VMEM((16, 16, 2, 128), F32),
            pltpu.VMEM((16, 2, 128), F32),
            pltpu.VMEM((16, 2, 128), F32),
            pltpu.VMEM((2, 128), F32),
            pltpu.VMEM((2, 16, 2, 128), F32),
            dma((40,)),
            dma((16, 2)),
            dma((16,)),
            dma(()),
            dma(()),
            dma((16,)),
            dma((16,)),
            dma((16,)),
            dma((16,)),
            dma((16,)),
            dma((16,)),
            dma((16,)),
            dma((16,)),
            dma((12,)),
            dma((12,)),
            dma(()),
            dma(()),
            dma((16,)),
            dma((16,)),
            dma((16,)),
            dma((16,)),
            dma((32,)),
            dma((2, 16)),
        ],
        compiler_params=pltpu.CompilerParams(
            collective_id=0, has_side_effects=True, vmem_limit_bytes=60 * 1024 * 1024
        ),
    )(
        query[0], passage[0], query_attn[0], passage_attn[0], negatives[0], positives,
        home[0].reshape(32, 128), down, up,
    )
    sums = res.reshape(2, 16, 256)
    return grad_q[None], grad_p[None], sums[0], sums[1]


def solution(mesh):
    in_specs = (
        P("fsdp", "dp", None),
        P("fsdp", "dp", None),
        P("fsdp", "dp", None),
        P("fsdp", "dp", None),
        P("fsdp", "dp"),
        P("fsdp", "dp", None),
        P("fsdp", None),
        P(None, "fsdp"),
        P(None, "fsdp"),
    )
    out_specs = (P("fsdp", "dp", None), P("fsdp", "dp", None), P(None, "fsdp"), P(None, "fsdp"))
    return jax.shard_map(
        per_device, mesh=mesh, in_specs=in_specs, out_specs=out_specs, check_vma=False
    )
```

```python
import jax
import jax.numpy as jnp
from jax import lax
from jax.experimental import pallas as pl
from jax.experimental.pallas import tpu as pltpu
from jax.sharding import PartitionSpec as P

MESH = pl.DeviceIdType.MESH
F32, BF16, I32 = jnp.float32, jnp.bfloat16, jnp.int32
HEAT = 100.0
ADAPTER_SCALE = 2.0
EPSILON = 1e-06
D = 4096
H = 2048
T = 512
NN = (((1,), (0,)), ((), ()))
NT = (((1,), (1,)), ((), ()))


def dot(lhs, rhs, dims=NN):
    return lax.dot_general(lhs, rhs, dims, preferred_element_type=F32)


def hi_lo(w):
    hi = w.astype(BF16)
    return hi, (w - hi.astype(F32)).astype(BF16)


def lanes_sum(v):
    return jnp.sum(v, axis=-1, keepdims=True)


def kernel(
    q_hbm, p_hbm, aq_hbm, ap_hbm, neg_hbm, home_hbm, aw_hbm, bw_hbm, pos_ref,
    gq_hbm, gp_hbm, down_hbm, up_hbm,
    q_ref, p_ref, aq_ref, ap_ref, neg_ref, home_ref, aw_ref, bw_ref, gq_ref, gp_ref, dv,
    qown, qoth, pb, ab, negp, lhs, rhs, csnd, crcv, ct, est, stat, srcv, rows_s,
    wt, woth, wq, gsnd, grcv, ysnd, yrcv,
    t1, rl1, d1p, d1m, r1m, r1p, uf, v1, t2, rl2, d2p, d2m, r2m, r2p,
    pup, dsum, dbuf, drow, rrow, zrow, zbuf, orow, oall,
    in_s, out_s, ag_s, q_r, qo_r, p_s, p_r, ab_s, ab_r, c_s, c_r, s_s, s_r, w_s, w_r, g_s, g_r, y_s, y_r,
    rs_s, rs_r, d_s, d_r, rr_s, rr_r, z_s, z_r, o_s, o_r,
):
    dp, z = lax.axis_index("dp"), lax.axis_index("fsdp")
    core, chip = lax.rem(dp, 2), dp // 2
    x, y = chip // 4, lax.rem(chip, 4)
    a = x * (1 - core) + y * core
    b = y * (1 - core) + x * core
    sa, sb = 8 - 6 * core, 2 + 6 * core
    other = 1 - core

    def near(v, k):
        return lax.rem(v + k, 4)

    def at(a_, b_):
        return (a_ * sa + b_ * sb + core, z)

    def slot(a_, b_):
        return b_ * 4 + a_

    me = slot(a, b)
    partner = (chip * 2 + other, z)
    am, a2, ap = near(a, 3), near(a, 2), near(a, 1)
    bm, b2, bp = near(b, 3), near(b, 2), near(b, 1)

    barrier = pltpu.get_barrier_semaphore()

    @pl.loop(1, 32)
    def _(k):
        pl.semaphore_signal(barrier, inc=1, device_id=(lax.rem(dp + k, 32), z), device_id_type=MESH)

    @pl.loop(1, 16)
    def _(k):
        pl.semaphore_signal(barrier, inc=1, device_id=(dp, lax.rem(z + k, 16)), device_id_type=MESH)

    loads = [
        pltpu.make_async_copy(src, dst, in_s.at[i])
        for i, (src, dst) in enumerate(
            (
                (q_hbm, q_ref), (p_hbm, p_ref), (aw_hbm, aw_ref), (bw_hbm, bw_ref),
                (neg_hbm, neg_ref), (home_hbm, home_ref), (aq_hbm, aq_ref), (ap_hbm, ap_ref),
            )
        )
    ]
    for c in loads:
        c.start()

    loads[0].wait()
    qv = q_ref[...].astype(F32)
    q_inv = 1.0 / jnp.sqrt(lanes_sum(qv * qv) + EPSILON)
    qe = (qv * q_inv).astype(BF16)
    qown[me, 0] = qe[:, :H]
    qown[me, 1] = qe[:, H:]
    for i in (2, 3):
        loads[i].wait()
    zcols = pl.ds(pl.multiple_of(z * 256, 256), 256)
    ab[0:16, zcols] = aw_ref[...]
    ab[16:32, zcols] = bw_ref[...]
    loads[1].wait()

    def p_rows(i, carry):
        rows = pl.ds(pl.multiple_of(i * 32, 32), 32)
        pv = p_ref[rows, :].astype(F32)
        p_len = jnp.sqrt(lanes_sum(pv * pv) + EPSILON)
        dst = pl.ds(pl.multiple_of(core * 128 + i * 32, 32), 32)
        pb[dst, :] = (pv * (1.0 / p_len)).astype(BF16)
        return carry

    lax.fori_loop(0, 4, p_rows, 0)

    pl.semaphore_wait(barrier, 46)

    sent = []

    def push(src, dst, ssem, rsem, device):
        c = pltpu.make_async_remote_copy(
            src_ref=src, dst_ref=dst, send_sem=ssem, recv_sem=rsem, device_id=device, device_id_type=MESH
        )
        c.start()
        return c

    def arrive(dst, rsem, ssem):
        pltpu.make_async_remote_copy(
            src_ref=dst, dst_ref=dst, send_sem=ssem, recv_sem=rsem, device_id=partner, device_id_type=MESH
        ).wait_recv()

    def gone(src, ssem, rsem):
        pltpu.make_async_remote_copy(
            src_ref=src, dst_ref=src, send_sem=ssem, recv_sem=rsem, device_id=partner, device_id_type=MESH
        ).wait_send()

    def peers(body):
        def one(k):
            a_, b_ = near(a, lax.rem(6 - lax.rem(k, 4), 4)), near(b, lax.rem(6 - k // 4, 4))
            body(a_, b_, slot(a_, b_))

        pl.loop(0, 10)(one)
        pl.loop(11, 16)(one)

    def q_full(s, device):
        n = len(sent)
        sent.append(push(qown.at[s], qown.at[s], ag_s.at[n], q_r.at[s, 0], device))

    def q_half(s, h, device):
        n = len(sent)
        sent.append(push(qown.at[s, h], qown.at[s, h], ag_s.at[n], q_r.at[s, h], device))

    def q_other(s):
        n = len(sent)
        sent.append(push(qown.at[s], qoth.at[s], ag_s.at[n], qo_r.at[s], partner))

    def got_full(s):
        arrive(qown.at[s], q_r.at[s, 0], ag_s.at[0])

    def got_halves(s):
        arrive(qown.at[s, 0], q_r.at[s, 0], ag_s.at[0])
        arrive(qown.at[s, 1], q_r.at[s, 1], ag_s.at[0])

    q_full(me, at(ap, b))
    q_full(me, at(am, b))
    q_full(me, at(a, bp))
    q_full(me, at(a, bm))
    own_rows = pl.ds(pl.multiple_of(core * 128, 128), 128)
    other_rows = pl.ds(pl.multiple_of(other * 128, 128), 128)
    p_copy = push(pb.at[own_rows], pb.at[own_rows], p_s, p_r, partner)
    q_other(me)

    @pl.loop(1, 16)
    def _(k):
        push(ab.at[:, zcols], ab.at[:, zcols], ab_s.at[k], ab_r.at[z], (dp, lax.rem(z + k, 16)))

    loads[4].wait()
    loads[5].wait()
    negp[...] = jnp.full((16, 128), -1, I32)
    negp[:, 0:64] = neg_ref[...]
    n_row = jnp.concatenate([negp[k : k + 1, :] for k in range(16)], axis=1)
    home = home_ref[...]
    table = jnp.concatenate(
        [(home >> 7).astype(F32).T, (home & 127).astype(F32).T], axis=0
    ).astype(BF16)
    for part in range(4):
        n = n_row[:, part * T : (part + 1) * T]
        lane_q = (lax.broadcasted_iota(I32, (1, T), 1) >> 7) + part * 4
        picked = (lax.broadcasted_iota(I32, (32, T), 0) == (n >> 7)).astype(F32).astype(BF16)
        found = dot(table, picked)
        low = lax.broadcasted_iota(I32, (128, T), 0) == (n & 127)
        dev_row = jnp.sum(jnp.where(low, found[0:128], 0.0), axis=0, keepdims=True).astype(I32)
        in_dev = jnp.sum(jnp.where(low, found[128:256], 0.0), axis=0, keepdims=True).astype(I32)
        chip_row = dev_row >> 1
        key = ((chip_row >> 2) * (1 + 3 * core) + (chip_row & 3) * (4 - 3 * core)) * 16 + lane_q
        key = jnp.where(n >= 0, key, -1)
        col = (dev_row & 1) * 128 + in_dev
        rows = lax.broadcasted_iota(I32, (256, T), 0)
        lhs[:, part * T : (part + 1) * T] = (rows == key).astype(F32).astype(BF16)
        rhs[:, part * T : (part + 1) * T] = (rows == col).astype(F32).astype(BF16)
    times = dot(lhs[...], rhs[...], NT).astype(BF16)
    csnd[:, 0] = times[:, 0:128].reshape(16, 16, 128)
    csnd[:, 1] = times[:, 128:256].reshape(16, 16, 128)
    crcv[me] = csnd[me]
    peers(lambda a_, b_, s: push(csnd.at[s], crcv.at[me], c_s.at[s], c_r.at[me], at(a_, b_)))
    lane = lax.broadcasted_iota(I32, (1, 64), 1)
    pos_row = jnp.full((1, 64), -1000, I32)
    for k in range(16):
        pos_row = jnp.where(lane == a * 16 + k, pos_ref[0, k], pos_row)
    pos_hot = (lax.broadcasted_iota(I32, (256, 64), 0) == pos_row + core * 128).astype(F32)
    own_lane = lax.broadcasted_iota(I32, (16, 64), 1) == a * 16 + lax.broadcasted_iota(I32, (16, 64), 0)

    def counts_ready():
        peers(lambda a_, b_, s: arrive(crcv.at[s], c_r.at[s], c_s.at[0]))
        for i in range(4):
            for k in range(2):
                ct[i, k * 128 : (k + 1) * 128, :] = (
                    crcv[i * 4 : i * 4 + 4, k].astype(F32).reshape(64, 128).T
                )
        ct[b] = ct[b] + pos_hot

    def scores(*blocks):
        def rows_of(h):
            got = [qown[pl.ds(b_ * 4, 4), h].reshape(64, H) for b_ in blocks]
            return got[0] if len(got) == 1 else jnp.concatenate(got, axis=0)

        s = dot(pb[:, 0:H], rows_of(0), NT)
        s = (s + dot(pb[:, H:D], rows_of(1), NT)) * HEAT
        return [s[:, i * 64 : (i + 1) * 64] for i in range(len(blocks))]

    def statistics(b_, s):
        c = ct[b_]
        named = c > 0.0
        top = jnp.max(jnp.where(named, s, -1e30), axis=0, keepdims=True)
        e = c * jnp.exp(jnp.where(named, s - top, -1e30))
        est[b_] = e
        stat[b_, 0:1, 0:64] = top
        stat[b_, 1:2, 0:64] = jnp.sum(e, axis=0, keepdims=True)
        stat[b_, 2:3, 0:64] = jnp.sum(e * s, axis=0, keepdims=True)

    got_full(slot(am, b))
    q_half(slot(am, b), 0, at(ap, b))
    q_full(slot(am, b), at(a, bp))
    q_full(slot(am, b), at(a, bm))
    got_full(slot(ap, b))
    q_half(slot(ap, b), 1, at(am, b))
    q_full(slot(ap, b), at(a, bp))
    q_full(slot(ap, b), at(a, bm))
    q_other(slot(am, b))
    q_other(slot(ap, b))
    got_full(slot(a, bm))
    q_half(slot(a, bm), 0, at(a, bp))
    got_full(slot(a, bp))
    q_half(slot(a, bp), 1, at(a, bm))
    got_halves(slot(a2, b))
    q_full(slot(a2, b), at(a, bp))
    q_full(slot(a2, b), at(a, bm))
    for a_ in (am, ap):
        got_full(slot(a_, bm))
        q_half(slot(a_, bm), 0, at(a, bp))
        got_full(slot(a_, bp))
        q_half(slot(a_, bp), 1, at(a, bm))
    q_other(slot(a2, b))
    for a_ in (a, am, ap):
        q_other(slot(a_, bm))
        q_other(slot(a_, bp))
    arrive(pb.at[other_rows], p_r, p_s)
    (s_b,) = scores(b)
    got_full(slot(a2, bm))
    q_half(slot(a2, bm), 0, at(a, bp))
    got_full(slot(a2, bp))
    q_half(slot(a2, bp), 1, at(a, bm))
    q_other(slot(a2, bm))
    q_other(slot(a2, bp))
    counts_ready()
    s_pos = jnp.sum(pos_hot * s_b, axis=0, keepdims=True)
    statistics(b, s_b)
    s_m, s_p = scores(bm, bp)
    statistics(bm, s_m)
    statistics(bp, s_p)
    for a_ in (a, am, ap, a2):
        got_halves(slot(a_, b2))
    (s_2,) = scores(b2)
    statistics(b2, s_2)
    peers(lambda a_, b_, s: push(stat, srcv.at[me], s_s.at[s], s_r.at[me], at(a_, b_)))
    srcv[me] = stat[...]
    for a_ in (a, am, ap, a2):
        q_other(slot(a_, b2))

    @pl.loop(1, 16)
    def _(k):
        zk = lax.rem(z + k, 16)
        cols = pl.ds(pl.multiple_of(zk * 256, 256), 256)
        arrive(ab.at[:, cols], ab_r.at[zk], ab_s.at[1])

    loads[6].wait()
    loads[7].wait()
    low_rows = dot(aq_ref[...], ab[0:16, :], NT).astype(BF16).astype(F32) * q_inv
    g_hi, g_lo = hi_lo(low_rows)
    gsnd[...] = jnp.zeros((16, 128), BF16)
    gsnd[:, 0:16] = g_hi
    gsnd[:, 16:32] = g_lo
    grcv[me] = gsnd[...]
    peers(lambda a_, b_, s: push(gsnd, grcv.at[me], g_s.at[s], g_r.at[me], at(a_, b_)))
    low_p = dot(ab[0:16, :], ap_ref[...], NT).astype(BF16)
    low_q = dot(ab[0:16, :], aq_ref[...], NT).astype(BF16)
    pbt = jnp.concatenate(hi_lo(dot(ab[16:32, :], pb[...], NT)), axis=0)
    block = pl.ds(b * 4, 4)
    ubt = dot(ab[16:32, 0:H], qown[block, 0].reshape(64, H), NT)
    ubt = ubt + dot(ab[16:32, H:D], qown[block, 1].reshape(64, H), NT)
    inv_row = jnp.sum(jnp.where(own_lane, q_inv, 0.0), axis=0, keepdims=True)

    peers(lambda a_, b_, s: arrive(srcv.at[s], s_r.at[s], s_s.at[0]))

    top = srcv[0, :, 0:1, :]
    for s in range(1, 16):
        top = jnp.maximum(top, srcv[s, :, 0:1, :])
    total = jnp.zeros((4, 1, 128), F32)
    first = jnp.zeros((4, 1, 128), F32)
    for s in range(16):
        f = jnp.exp(srcv[s, :, 0:1, :] - top)
        total = total + f * srcv[s, :, 1:2, :]
        first = first + f * srcv[s, :, 2:3, :]
    rows_s[:, 0:1, :] = jnp.exp(stat[:, 0:1, :] - top) * (HEAT / total)
    rows_s[:, 1:2, :] = first / total
    for i in range(4):
        est[i] = est[i] * rows_s[i, 0:1, 0:64]
    est[b] = est[b] - HEAT * pos_hot
    weight = jnp.concatenate([est[i] for i in range(4)], axis=1)
    w_hi, w_lo = hi_lo(weight)
    wt[0] = w_hi
    wt[1] = w_lo
    w_copy = push(wt.at[:, other_rows], woth, w_s, w_r, partner)
    inner_row = rows_s[b, 1:2, 0:64] - s_pos
    inner = lanes_sum(jnp.where(own_lane, inner_row, 0.0))

    for i in range(4):
        cols = slice(i * 64, (i + 1) * 64)
        share = dot(pbt, w_hi[:, cols]) + dot(pbt, w_lo[:, cols])
        ysnd[i, :, 0:64] = share[0:16] + share[16:32]
    peers(lambda a_, b_, s: push(ysnd.at[b_], yrcv.at[me], y_s.at[s], y_r.at[me], at(a_, b_)))
    yrcv[me] = ysnd[b]
    wq_hi, wq_lo = hi_lo(weight.T)
    wq[0] = wq_hi
    wq[1] = wq_lo

    def shares(b_, h, put):
        rows = pl.ds(pl.multiple_of(b_ * 64, 64), 64)
        w = jnp.concatenate([wq[0, rows, :], wq[1, rows, :]], axis=0)
        for j in range(H // T):
            r = dot(w, pb[:, h * H + j * T : h * H + (j + 1) * T])
            put(slice(j * T, (j + 1) * T), (r[0:64] + r[64:128]).reshape(4, 16, T))

    def put_in(ref, *where):
        def put(cols, r):
            ref[(*where, slice(None), slice(None), cols)] = r.astype(ref.dtype)

        return put

    rs = []

    def hop(src, dst, device):
        n = len(rs)
        rs.append(push(src, dst, rs_s.at[n], rs_r.at[n], device))

    def landed(dst, n):
        arrive(dst, rs_r.at[n], rs_s.at[0])

    shares(b2, 0, put_in(t1, 0))
    hop(t1.at[0], rl1.at[0], at(a, bp))
    shares(b2, 1, put_in(t1, 1))
    hop(t1.at[1], rl1.at[1], at(a, bm))
    shares(bp, 1, put_in(d1p, 1))
    hop(d1p.at[1], r1m.at[1], at(a, bp))
    shares(bm, 0, put_in(d1m, 0))
    hop(d1m.at[0], r1p.at[0], at(a, bm))

    for a_, b_ in ((am, b), (ap, b), (a2, b), (a, bm), (a, bp), (a, b)):
        arrive(qoth.at[slot(a_, b_)], qo_r.at[slot(a_, b_)], ag_s.at[0])
    for a_ in (am, ap, a2):
        for b_ in (bm, bp):
            arrive(qoth.at[slot(a_, b_)], qo_r.at[slot(a_, b_)], ag_s.at[0])
    for a_ in (a, am, ap, a2):
        arrive(qoth.at[slot(a_, b2)], qo_r.at[slot(a_, b2)], ag_s.at[0])
    arrive(woth, w_r, w_s)
    wa = jnp.concatenate([wt[0, own_rows, :], wt[1, own_rows, :]], axis=0)
    wb = jnp.concatenate([woth[0], woth[1]], axis=0)
    p_sq = jnp.zeros((128, 1), F32)
    p_in = jnp.zeros((128, 1), F32)
    for h in range(2):
        for j in range(H // T):
            cols = slice(h * H + j * T, h * H + (j + 1) * T)
            sub = slice(j * T, (j + 1) * T)
            r = dot(wa, qown[:, h, :, sub].reshape(256, T))
            r = r + dot(wb, qoth[:, h, :, sub].reshape(256, T))
            r = r[0:128] + r[128:256]
            pv = p_ref[:, cols].astype(F32)
            p_sq = p_sq + lanes_sum(pv * pv)
            p_in = p_in + lanes_sum(pv * r)
            pup[:, cols] = r
    p_inv = 1.0 / jnp.sqrt(p_sq + EPSILON)
    p_in = p_in * p_inv * p_inv
    for j in range(D // T):
        cols = slice(j * T, (j + 1) * T)
        gp_ref[:, cols] = ((pup[:, cols] - p_ref[:, cols].astype(F32) * p_in) * p_inv).astype(BF16)
    gp_out = pltpu.make_async_copy(gp_ref, gp_hbm, out_s.at[0])
    gp_out.start()

    back_p = dot(ab[16:32, :], gp_ref[...], NT).astype(BF16)
    peers(lambda a_, b_, s: arrive(grcv.at[s], g_r.at[s], g_s.at[0]))
    gall = grcv[...].reshape(256, 128)
    xt = (dot(wt[0], gall) + dot(wt[1], gall)).T
    xs = jnp.concatenate(hi_lo(xt[0:16] + xt[16:32]), axis=0)
    peers(lambda a_, b_, s: arrive(yrcv.at[s], y_r.at[s], y_s.at[0]))
    ysum = yrcv[0, :, 0:64]
    for s in range(1, 16):
        ysum = ysum + yrcv[s, :, 0:64]
    back = ((ysum - inner_row * ubt) * inv_row).astype(BF16)
    pick = lax.broadcasted_iota(I32, (64, 16), 0) == a * 16 + lax.broadcasted_iota(I32, (64, 16), 1)
    back_q = dot(back, pick.astype(F32).astype(BF16)).astype(BF16)
    for j in range(D // T):
        cols = slice(j * T, (j + 1) * T)
        r = dot(back_p, ap_ref[:, cols]) + dot(back_q, aq_ref[:, cols])
        dsum[0:16, cols] = ADAPTER_SCALE * r
        v2 = (q_ref[:, cols].astype(F32) * (inner * q_inv * q_inv)).astype(BF16)
        r = dot(xs, pb[:, cols])
        r = r[0:16] + r[16:32] + dot(low_p, gp_ref[:, cols]) - dot(low_q, v2)
        dsum[16:32, cols] = ADAPTER_SCALE * r
    mine = pl.ds(pl.multiple_of(core * 16, 16), 16)
    theirs = pl.ds(pl.multiple_of(other * 16, 16), 16)
    d_copy = push(dsum.at[theirs], dbuf, d_s, d_r, partner)

    shares(bp, 0, put_in(uf, 0))
    landed(rl1.at[0], 0)
    d1p[0] = (uf[0] + rl1[0].astype(F32)).astype(BF16)
    hop(d1p.at[0], r1m.at[0], at(a, bp))
    shares(bm, 1, put_in(uf, 1))
    landed(rl1.at[1], 1)
    d1m[1] = (uf[1] + rl1[1].astype(F32)).astype(BF16)
    hop(d1m.at[1], r1p.at[1], at(a, bm))

    arrive(dbuf, d_r, d_s)
    for j in range(D // 128):
        cols = slice(j * 128, (j + 1) * 128)
        drow[:, j // 2, j % 2, :] = dsum[mine, cols] + dbuf[:, cols]
    peers(lambda a_, b_, s: push(drow.at[s], rrow.at[me], rr_s.at[s], rr_r.at[me], at(a_, b_)))
    rrow[me] = drow[me]
    shares(b, 0, put_in(v1, 0))
    shares(b, 1, put_in(v1, 1))
    peers(lambda a_, b_, s: arrive(rrow.at[s], rr_r.at[s], rr_s.at[0]))
    acc = rrow[0]
    for s in range(1, 16):
        acc = acc + rrow[s]
    zrow[...] = acc

    @pl.loop(0, 15)
    def _(k):
        zk = lax.rem(z + lax.rem(k + 4, 15) + 1, 16)
        push(zrow.at[zk], zbuf.at[z], z_s.at[zk], z_r.at[z], (dp, zk))

    zbuf[z] = zrow[z]

    landed(r1m.at[1], 2)
    landed(r1p.at[0], 3)
    landed(r1m.at[0], 4)
    landed(r1p.at[1], 5)
    for h in range(2):
        v1[h] = v1[h] + r1m[h].astype(F32) + r1p[h].astype(F32)
        t2[h] = v1[h, a2].astype(BF16)
        if h == 0:
            hop(t2.at[0], rl2.at[0], at(ap, b))
            d2m[0] = v1[0, am].astype(BF16)
            hop(d2m.at[0], r2p.at[0], at(am, b))
        else:
            hop(t2.at[1], rl2.at[1], at(am, b))
            d2p[1] = v1[1, ap].astype(BF16)
            hop(d2p.at[1], r2m.at[1], at(ap, b))
    landed(rl2.at[0], 6)
    d2p[0] = (v1[0, ap] + rl2[0].astype(F32)).astype(BF16)
    hop(d2p.at[0], r2m.at[0], at(ap, b))
    landed(rl2.at[1], 8)
    d2m[1] = (v1[1, am] + rl2[1].astype(F32)).astype(BF16)
    hop(d2m.at[1], r2p.at[1], at(am, b))

    @pl.loop(1, 16)
    def _(k):
        zk = lax.rem(z + k, 16)
        arrive(zbuf.at[zk], z_r.at[zk], z_s.at[0])

    acc = zbuf[0]
    for s in range(1, 16):
        acc = acc + zbuf[s]
    orow[...] = acc
    oall[core, me] = acc

    @pl.loop(1, 32)
    def _(k):
        push(orow, oall.at[core, me], o_s.at[k], o_r.at[core, me], (lax.rem(dp + k, 32), z))

    landed(r2p.at[0], 7)
    landed(r2m.at[1], 9)
    landed(r2m.at[0], 10)
    landed(r2p.at[1], 11)
    qu = jnp.concatenate(
        [v1[h, a] + r2m[h].astype(F32) + r2p[h].astype(F32) for h in range(2)], axis=1
    )
    qv = q_ref[...].astype(F32)
    q_inv = 1.0 / jnp.sqrt(lanes_sum(qv * qv) + EPSILON)
    q_in = lanes_sum(qv * qu) * q_inv * q_inv
    gq_ref[...] = ((qu - qv * q_in) * q_inv).astype(BF16)
    gq_out = pltpu.make_async_copy(gq_ref, gq_hbm, out_s.at[1])
    gq_out.start()

    for c in sent + rs + [p_copy, d_copy, w_copy]:
        c.wait_send()

    @pl.loop(1, 16)
    def _(k):
        a_, b_ = near(a, lax.rem(k, 4)), near(b, k // 4)
        s = slot(a_, b_)
        gone(csnd.at[s], c_s.at[s], c_r.at[s])
        gone(stat, s_s.at[s], s_r.at[s])
        gone(gsnd, g_s.at[s], g_r.at[s])
        gone(ysnd.at[b_], y_s.at[s], y_r.at[s])
        gone(drow.at[s], rr_s.at[s], rr_r.at[s])
        zk = lax.rem(z + k, 16)
        gone(zrow.at[zk], z_s.at[zk], z_r.at[zk])
        gone(ab.at[:, zcols], ab_s.at[k], ab_r.at[z])

    @pl.loop(1, 32)
    def _(k):
        d_ = lax.rem(dp + k, 32)
        c_, h_ = lax.rem(d_, 2), d_ // 2
        s_ = (h_ // 4) * (1 + 3 * c_) + lax.rem(h_, 4) * (4 - 3 * c_)
        arrive(oall.at[c_, s_], o_r.at[c_, s_], o_s.at[1])

    outs = [gp_out, gq_out]
    for c_, dst in ((0, down_hbm), (1, up_hbm)):
        dv[c_, :, 0:128] = oall[c_, :, 0, :]
        dv[c_, :, 128:256] = oall[c_, :, 1, :]
        outs.append(pltpu.make_async_copy(dv.at[c_], dst, out_s.at[2 + c_]))
        outs[-1].start()

    @pl.loop(1, 32)
    def _(k):
        gone(orow, o_s.at[k], o_r.at[0, 0])

    for c in outs:
        c.wait()


ANY = pl.BlockSpec(memory_space=pl.ANY)
SM = pl.BlockSpec(memory_space=pltpu.SMEM)


def per_device(query, passage, query_attn, passage_attn, positives, negatives, home, down, up):
    dma = pltpu.SemaphoreType.DMA
    vm = pltpu.VMEM
    half = vm((2, 4, 16, H), BF16)
    row = vm((2, 16, H), BF16)
    grad_q, grad_p, sum_down, sum_up = pl.pallas_call(
        kernel,
        out_shape=(
            jax.ShapeDtypeStruct((16, D), BF16),
            jax.ShapeDtypeStruct((128, D), BF16),
            jax.ShapeDtypeStruct((16, 256), F32),
            jax.ShapeDtypeStruct((16, 256), F32),
        ),
        in_specs=[ANY] * 8 + [SM],
        out_specs=(ANY,) * 4,
        scratch_shapes=[
            vm((16, D), BF16),
            vm((128, D), BF16),
            vm((16, D), BF16),
            vm((128, D), BF16),
            vm((16, 64), I32),
            vm((32, 128), I32),
            vm((16, 256), BF16),
            vm((16, 256), BF16),
            vm((16, D), BF16),
            vm((128, D), BF16),
            vm((2, 16, 256), F32),
            vm((16, 2, 16, H), BF16),
            vm((16, 2, 16, H), BF16),
            vm((256, D), BF16),
            vm((32, D), BF16),
            vm((16, 128), I32),
            vm((256, H), BF16),
            vm((256, H), BF16),
            vm((16, 2, 16, 128), BF16),
            vm((16, 2, 16, 128), BF16),
            vm((4, 256, 64), F32),
            vm((4, 256, 64), F32),
            vm((4, 4, 128), F32),
            vm((16, 4, 4, 128), F32),
            vm((4, 4, 128), F32),
            vm((2, 256, 256), BF16),
            vm((2, 128, 256), BF16),
            vm((2, 256, 256), BF16),
            vm((16, 128), BF16),
            vm((16, 16, 128), BF16),
            vm((4, 16, 128), F32),
            vm((16, 16, 128), F32),
            half,
            half,
            half,
            half,
            half,
            half,
            vm((2, 4, 16, H), F32),
            vm((2, 4, 16, H), F32),
            row,
            row,
            row,
            row,
            row,
            row,
            vm((128, D), F32),
            vm((32, D), F32),
            vm((16, D), F32),
            vm((16, 16, 2, 128), F32),
            vm((16, 16, 2, 128), F32),
            vm((16, 2, 128), F32),
            vm((16, 2, 128), F32),
            vm((2, 128), F32),
            vm((2, 16, 2, 128), F32),
            dma((8,)),
            dma((4,)),
            dma((40,)),
            dma((16, 2)),
            dma((16,)),
            dma(()),
            dma(()),
            dma((16,)),
            dma((16,)),
            dma((16,)),
            dma((16,)),
            dma((16,)),
            dma((16,)),
            dma(()),
            dma(()),
            dma((16,)),
            dma((16,)),
            dma((16,)),
            dma((16,)),
            dma((12,)),
            dma((12,)),
            dma(()),
            dma(()),
            dma((16,)),
            dma((16,)),
            dma((16,)),
            dma((16,)),
            dma((32,)),
            dma((2, 16)),
        ],
        compiler_params=pltpu.CompilerParams(
            collective_id=0, has_side_effects=True, vmem_limit_bytes=60 * 1024 * 1024
        ),
    )(
        query[0], passage[0], query_attn[0], passage_attn[0], negatives[0],
        home[0].reshape(32, 128), down, up, positives,
    )
    return grad_q[None], grad_p[None], sum_down, sum_up


def solution(mesh):
    in_specs = (
        P("fsdp", "dp", None),
        P("fsdp", "dp", None),
        P("fsdp", "dp", None),
        P("fsdp", "dp", None),
        P("fsdp", "dp"),
        P("fsdp", "dp", None),
        P("fsdp", None),
        P(None, "fsdp"),
        P(None, "fsdp"),
    )
    out_specs = (P("fsdp", "dp", None), P("fsdp", "dp", None), P(None, "fsdp"), P(None, "fsdp"))
    return jax.shard_map(
        per_device, mesh=mesh, in_specs=in_specs, out_specs=out_specs, check_vma=False
    )
```

```python
import jax
import jax.numpy as jnp
from jax import lax
from jax.experimental import pallas as pl
from jax.experimental.pallas import tpu as pltpu
from jax.sharding import PartitionSpec as P

MESH = pl.DeviceIdType.MESH
F32, BF16, I32 = jnp.float32, jnp.bfloat16, jnp.int32
HEAT = 100.0
ADAPTER_SCALE = 2.0
EPSILON = 1e-06
D = 4096
H = 2048
T = 512
NN = (((1,), (0,)), ((), ()))
NT = (((1,), (1,)), ((), ()))


def dot(lhs, rhs, dims=NN):
    return lax.dot_general(lhs, rhs, dims, preferred_element_type=F32)


def hi_lo(w):
    hi = w.astype(BF16)
    return hi, (w - hi.astype(F32)).astype(BF16)


def lanes_sum(v):
    return jnp.sum(v, axis=-1, keepdims=True)


def kernel(
    q_hbm, p_hbm, aq_hbm, ap_hbm, neg_hbm, home_hbm, aw_hbm, bw_hbm, pos_hbm,
    gq_hbm, gp_hbm, down_hbm, up_hbm,
    q_ref, p_ref, aq_ref, ap_ref, neg_ref, home_ref, aw_ref, bw_ref, pos_ref, gq_ref, gp_ref, dv,
    qown, qoth, pb, ab, negp, lhs, rhs, csnd, crcv, ct, est, stat, srcv, rows_s,
    wt, woth, wq, gsnd, grcv, ysnd, yrcv,
    t1, rl1, d1p, d1m, r1m, r1p, uf, v1, t2, rl2, d2p, d2m, r2m, r2p,
    pinv, pup, dsum, dbuf, drow, rrow, zrow, zbuf, orow, oall,
    in_s, out_s, ag_s, q_r, qo_r, p_s, p_r, ab_s, ab_r, c_s, c_r, s_s, s_r, w_s, w_r, g_s, g_r, y_s, y_r,
    rs_s, rs_r, d_s, d_r, rr_s, rr_r, z_s, z_r, o_s, o_r,
):
    dp, z = lax.axis_index("dp"), lax.axis_index("fsdp")
    core, chip = lax.rem(dp, 2), dp // 2
    x, y = chip // 4, lax.rem(chip, 4)
    a = x * (1 - core) + y * core
    b = y * (1 - core) + x * core
    sa, sb = 8 - 6 * core, 2 + 6 * core
    other = 1 - core

    def near(v, k):
        return lax.rem(v + k, 4)

    def at(a_, b_):
        return (a_ * sa + b_ * sb + core, z)

    def slot(a_, b_):
        return b_ * 4 + a_

    me = slot(a, b)
    partner = (chip * 2 + other, z)
    am, a2, ap = near(a, 3), near(a, 2), near(a, 1)
    bm, b2, bp = near(b, 3), near(b, 2), near(b, 1)

    barrier = pltpu.get_barrier_semaphore()

    loads = [
        pltpu.make_async_copy(src, dst, in_s.at[i])
        for i, (src, dst) in enumerate(
            (
                (q_hbm, q_ref), (p_hbm, p_ref), (aw_hbm, aw_ref), (bw_hbm, bw_ref),
                (neg_hbm, neg_ref), (home_hbm, home_ref), (aq_hbm, aq_ref), (ap_hbm, ap_ref), (pos_hbm, pos_ref),
            )
        )
    ]
    loads[0].start()
    loads[1].start()

    @pl.loop(1, 32)
    def _(k):
        pl.semaphore_signal(barrier, inc=1, device_id=(lax.rem(dp + k, 32), z), device_id_type=MESH)

    @pl.loop(1, 16)
    def _(k):
        pl.semaphore_signal(barrier, inc=1, device_id=(dp, lax.rem(z + k, 16)), device_id_type=MESH)

    for c in loads[2:]:
        c.start()

    loads[0].wait()
    qv = q_ref[...].astype(F32)
    q_inv = 1.0 / jnp.sqrt(lanes_sum(qv * qv) + EPSILON)
    qe = (qv * q_inv).astype(BF16)
    qown[me, 0] = qe[:, :H]
    qown[me, 1] = qe[:, H:]
    for i in (2, 3):
        loads[i].wait()
    zcols = pl.ds(pl.multiple_of(z * 256, 256), 256)
    ab[0:16, zcols] = aw_ref[...]
    ab[16:32, zcols] = bw_ref[...]
    loads[1].wait()

    def p_rows(i, carry):
        rows = pl.ds(pl.multiple_of(i * 32, 32), 32)
        pv = p_ref[rows, :].astype(F32)
        inv = 1.0 / jnp.sqrt(lanes_sum(pv * pv) + EPSILON)
        pinv[rows, :] = jnp.broadcast_to(inv, (32, 128))
        dst = pl.ds(pl.multiple_of(core * 128 + i * 32, 32), 32)
        pb[dst, :] = (pv * inv).astype(BF16)
        return carry

    lax.fori_loop(0, 4, p_rows, 0)

    pl.semaphore_wait(barrier, 46)

    def push(src, dst, ssem, rsem, device):
        c = pltpu.make_async_remote_copy(
            src_ref=src, dst_ref=dst, send_sem=ssem, recv_sem=rsem, device_id=device, device_id_type=MESH
        )
        c.start()
        return c

    def arrive(dst, rsem, ssem):
        pltpu.make_async_remote_copy(
            src_ref=dst, dst_ref=dst, send_sem=ssem, recv_sem=rsem, device_id=partner, device_id_type=MESH
        ).wait_recv()

    def gone(src, ssem, rsem):
        pltpu.make_async_remote_copy(
            src_ref=src, dst_ref=src, send_sem=ssem, recv_sem=rsem, device_id=partner, device_id_type=MESH
        ).wait_send()

    def peers(body):
        def one(k):
            a_, b_ = near(a, lax.rem(6 - lax.rem(k, 4), 4)), near(b, lax.rem(6 - k // 4, 4))
            body(a_, b_, slot(a_, b_))

        pl.loop(0, 10)(one)
        pl.loop(11, 16)(one)

    def q_half(s, h, device):
        push(qown.at[s, h], qown.at[s, h], ag_s.at[0], q_r.at[s, h], device)

    def q_other(s):
        push(qown.at[s], qoth.at[s], ag_s.at[1], qo_r, partner)

    def got_half(s, h):
        arrive(qown.at[s, h], q_r.at[s, h], ag_s.at[0])

    q_half(me, 0, at(ap, b))
    q_half(me, 1, at(am, b))
    q_half(me, 1, at(ap, b))
    q_half(me, 0, at(am, b))
    own_rows = pl.ds(pl.multiple_of(core * 128, 128), 128)
    other_rows = pl.ds(pl.multiple_of(other * 128, 128), 128)
    p_copy = push(pb.at[own_rows], pb.at[own_rows], p_s, p_r, partner)
    q_other(me)

    @pl.loop(1, 16)
    def _(k):
        push(ab.at[:, zcols], ab.at[:, zcols], ab_s, ab_r, (dp, lax.rem(z + k, 16)))

    loads[4].wait()
    loads[5].wait()
    loads[8].wait()
    negp[...] = jnp.full((16, 128), -1, I32)
    negp[:, 0:64] = neg_ref[...]
    n_row = jnp.concatenate([negp[k : k + 1, :] for k in range(16)], axis=1)
    home = home_ref[...]
    table = jnp.concatenate(
        [(home >> 7).astype(F32).T, (home & 127).astype(F32).T], axis=0
    ).astype(BF16)
    for part in range(4):
        if part == 1:
            q_half(me, 0, at(a, bp))
            q_half(me, 1, at(a, bm))
            q_half(me, 1, at(a, bp))
            q_half(me, 0, at(a, bm))
        n = n_row[:, part * T : (part + 1) * T]
        lane_q = (lax.broadcasted_iota(I32, (1, T), 1) >> 7) + part * 4
        picked = (lax.broadcasted_iota(I32, (32, T), 0) == (n >> 7)).astype(F32).astype(BF16)
        found = dot(table, picked)
        low = lax.broadcasted_iota(I32, (128, T), 0) == (n & 127)
        dev_row = jnp.sum(jnp.where(low, found[0:128], 0.0), axis=0, keepdims=True).astype(I32)
        in_dev = jnp.sum(jnp.where(low, found[128:256], 0.0), axis=0, keepdims=True).astype(I32)
        chip_row = dev_row >> 1
        key = ((chip_row >> 2) * (1 + 3 * core) + (chip_row & 3) * (4 - 3 * core)) * 16 + lane_q
        key = jnp.where(n >= 0, key, -1)
        col = (dev_row & 1) * 128 + in_dev
        rows = lax.broadcasted_iota(I32, (256, T), 0)
        lhs[:, part * T : (part + 1) * T] = (rows == key).astype(F32).astype(BF16)
        rhs[:, part * T : (part + 1) * T] = (rows == col).astype(F32).astype(BF16)
    times = dot(lhs[...], rhs[...], NT).astype(BF16)
    csnd[:, 0] = times[:, 0:128].reshape(16, 16, 128)
    csnd[:, 1] = times[:, 128:256].reshape(16, 16, 128)
    crcv[me] = csnd[me]
    peers(lambda a_, b_, s: push(csnd.at[s], crcv.at[me], c_s, c_r, at(a_, b_)))
    lane = lax.broadcasted_iota(I32, (1, 64), 1)
    pos_row = jnp.full((1, 64), -1000, I32)
    for k in range(16):
        pos_row = jnp.where(lane == a * 16 + k, pos_ref[0, k], pos_row)
    pos_hot = (lax.broadcasted_iota(I32, (256, 64), 0) == pos_row + core * 128).astype(F32)
    own_lane = lax.broadcasted_iota(I32, (16, 64), 1) == a * 16 + lax.broadcasted_iota(I32, (16, 64), 0)

    def counts_ready():
        arrive(crcv.at[0:15], c_r, c_s)
        for i in range(4):
            for k in range(2):
                ct[i, k * 128 : (k + 1) * 128, :] = (
                    crcv[i * 4 : i * 4 + 4, k].astype(F32).reshape(64, 128).T
                )
        ct[b] = ct[b] + pos_hot

    def scores(*blocks):
        def rows_of(h):
            got = [qown[pl.ds(b_ * 4, 4), h].reshape(64, H) for b_ in blocks]
            return got[0] if len(got) == 1 else jnp.concatenate(got, axis=0)

        s = dot(pb[:, 0:H], rows_of(0), NT)
        s = (s + dot(pb[:, H:D], rows_of(1), NT)) * HEAT
        return [s[:, i * 64 : (i + 1) * 64] for i in range(len(blocks))]

    def statistics(b_, s):
        c = ct[b_]
        named = c > 0.0
        top = jnp.max(jnp.where(named, s, -1e30), axis=0, keepdims=True)
        e = c * jnp.exp(jnp.where(named, s - top, -1e30))
        est[b_] = e
        stat[b_, 0:1, 0:64] = top
        stat[b_, 1:2, 0:64] = jnp.sum(e, axis=0, keepdims=True)
        stat[b_, 2:3, 0:64] = jnp.sum(e * s, axis=0, keepdims=True)

    got_half(slot(am, b), 0)
    q_half(slot(am, b), 0, at(ap, b))
    q_half(slot(am, b), 0, at(a, bp))
    got_half(slot(ap, b), 1)
    q_half(slot(ap, b), 1, at(am, b))
    q_half(slot(ap, b), 1, at(a, bm))
    got_half(slot(am, b), 1)
    q_half(slot(am, b), 1, at(a, bm))
    q_half(slot(am, b), 1, at(a, bp))
    got_half(slot(ap, b), 0)
    q_half(slot(ap, b), 0, at(a, bp))
    q_half(slot(ap, b), 0, at(a, bm))
    q_half(slot(am, b), 0, at(a, bm))
    q_half(slot(ap, b), 1, at(a, bp))
    q_other(slot(am, b))
    q_other(slot(ap, b))
    got_half(slot(a, bm), 0)
    q_half(slot(a, bm), 0, at(a, bp))
    got_half(slot(a, bp), 1)
    q_half(slot(a, bp), 1, at(a, bm))
    got_half(slot(a2, b), 0)
    q_half(slot(a2, b), 0, at(a, bp))
    got_half(slot(a2, b), 1)
    q_half(slot(a2, b), 1, at(a, bm))
    q_half(slot(a2, b), 1, at(a, bp))
    q_half(slot(a2, b), 0, at(a, bm))
    q_other(slot(a2, b))
    arrive(pb.at[other_rows], p_r, p_s)
    (s_b,) = scores(b)
    for a_ in (am, ap):
        got_half(slot(a_, bm), 0)
        q_half(slot(a_, bm), 0, at(a, bp))
        got_half(slot(a_, bp), 1)
        q_half(slot(a_, bp), 1, at(a, bm))
    counts_ready()
    s_pos = jnp.sum(pos_hot * s_b, axis=0, keepdims=True)
    statistics(b, s_b)
    got_half(slot(a2, bm), 0)
    q_half(slot(a2, bm), 0, at(a, bp))
    got_half(slot(a2, bp), 1)
    q_half(slot(a2, bp), 1, at(a, bm))
    for a_ in (a, am, ap, a2):
        got_half(slot(a_, bm), 1)
        got_half(slot(a_, bp), 0)
        q_other(slot(a_, bm))
        q_other(slot(a_, bp))
    s_m, s_p = scores(bm, bp)
    statistics(bm, s_m)
    statistics(bp, s_p)
    for a_ in (a, am, ap, a2):
        for h in range(2):
            got_half(slot(a_, b2), h)
    (s_2,) = scores(b2)
    statistics(b2, s_2)
    peers(lambda a_, b_, s: push(stat, srcv.at[me], s_s, s_r, at(a_, b_)))
    srcv[me] = stat[...]
    for a_ in (a, am, ap, a2):
        q_other(slot(a_, b2))

    arrive(ab.at[:, 0 : 15 * 256], ab_r, ab_s)
    loads[6].wait()
    loads[7].wait()
    low_rows = dot(aq_ref[...], ab[0:16, :], NT).astype(BF16).astype(F32) * q_inv
    g_hi, g_lo = hi_lo(low_rows)
    gsnd[...] = jnp.zeros((16, 128), BF16)
    gsnd[:, 0:16] = g_hi
    gsnd[:, 16:32] = g_lo
    grcv[me] = gsnd[...]
    peers(lambda a_, b_, s: push(gsnd, grcv.at[me], g_s, g_r, at(a_, b_)))
    low_p = dot(ab[0:16, :], ap_ref[...], NT).astype(BF16)
    low_q = dot(ab[0:16, :], aq_ref[...], NT).astype(BF16)
    pbt = jnp.concatenate(hi_lo(dot(ab[16:32, :], pb[...], NT)), axis=0)
    block = pl.ds(b * 4, 4)
    ubt = dot(ab[16:32, 0:H], qown[block, 0].reshape(64, H), NT)
    ubt = ubt + dot(ab[16:32, H:D], qown[block, 1].reshape(64, H), NT)
    inv_row = jnp.sum(jnp.where(own_lane, q_inv, 0.0), axis=0, keepdims=True)

    arrive(srcv.at[0:15], s_r, s_s)

    top = srcv[0, :, 0:1, :]
    for s in range(1, 16):
        top = jnp.maximum(top, srcv[s, :, 0:1, :])
    total = jnp.zeros((4, 1, 128), F32)
    first = jnp.zeros((4, 1, 128), F32)
    for s in range(16):
        f = jnp.exp(srcv[s, :, 0:1, :] - top)
        total = total + f * srcv[s, :, 1:2, :]
        first = first + f * srcv[s, :, 2:3, :]
    rows_s[:, 0:1, :] = jnp.exp(stat[:, 0:1, :] - top) * (HEAT / total)
    rows_s[:, 1:2, :] = first / total
    for i in range(4):
        est[i] = est[i] * rows_s[i, 0:1, 0:64]
    est[b] = est[b] - HEAT * pos_hot
    weight = jnp.concatenate([est[i] for i in range(4)], axis=1)
    w_hi, w_lo = hi_lo(weight)
    wt[0] = w_hi
    wt[1] = w_lo
    w_copy = push(wt.at[:, other_rows], woth, w_s, w_r, partner)
    inner_row = rows_s[b, 1:2, 0:64] - s_pos
    inner = lanes_sum(jnp.where(own_lane, inner_row, 0.0))

    for i in range(4):
        cols = slice(i * 64, (i + 1) * 64)
        share = dot(pbt, w_hi[:, cols]) + dot(pbt, w_lo[:, cols])
        ysnd[i, :, 0:64] = share[0:16] + share[16:32]
    peers(lambda a_, b_, s: push(ysnd.at[b_], yrcv.at[me], y_s, y_r, at(a_, b_)))
    yrcv[me] = ysnd[b]
    arrive(grcv.at[0:15], g_r, g_s)
    gall = grcv[...].reshape(256, 128)
    xt = (dot(wt[0], gall) + dot(wt[1], gall)).T
    xs = jnp.concatenate(hi_lo(xt[0:16] + xt[16:32]), axis=0)

    wq_hi, wq_lo = hi_lo(weight.T)
    wq[0] = wq_hi
    wq[1] = wq_lo

    def shares(b_, h, put):
        rows = pl.ds(pl.multiple_of(b_ * 64, 64), 64)
        w = jnp.concatenate([wq[0, rows, :], wq[1, rows, :]], axis=0)
        for j in range(H // T):
            r = dot(w, pb[:, h * H + j * T : h * H + (j + 1) * T])
            put(slice(j * T, (j + 1) * T), (r[0:64] + r[64:128]).reshape(4, 16, T))

    def put_in(ref, *where):
        def put(cols, r):
            ref[(*where, slice(None), slice(None), cols)] = r.astype(ref.dtype)

        return put

    rs = []

    def hop(n, src, dst, device):
        rs.append(push(src, dst, rs_s.at[n], rs_r.at[n], device))

    def landed(dst, n):
        arrive(dst, rs_r.at[n], rs_s.at[0])

    shares(b2, 0, put_in(t1, 0))
    hop(0, t1.at[0], rl1.at[0], at(a, bp))
    shares(b2, 1, put_in(t1, 1))
    hop(1, t1.at[1], rl1.at[1], at(a, bm))

    def two_parts(w, q, h, sub):
        r = dot(w, q[:, h, :, sub].reshape(256, T))
        return r[0:128] + r[128:256]

    wa = jnp.concatenate([wt[0, own_rows, :], wt[1, own_rows, :]], axis=0)
    for h in range(2):
        for j in range(H // T):
            cols = slice(h * H + j * T, h * H + (j + 1) * T)
            pup[:, cols] = two_parts(wa, qown, h, slice(j * T, (j + 1) * T))
            r = dot(xs, pb[:, cols])
            dsum[16:32, cols] = r[0:16] + r[16:32]
    arrive(qoth, qo_r, ag_s.at[1])
    arrive(woth, w_r, w_s)
    wb = jnp.concatenate([woth[0], woth[1]], axis=0)
    p_in = jnp.zeros((128, 1), F32)
    for h in range(2):
        for j in range(H // T):
            cols = slice(h * H + j * T, h * H + (j + 1) * T)
            r = pup[:, cols] + two_parts(wb, qoth, h, slice(j * T, (j + 1) * T))
            p_in = p_in + lanes_sum(p_ref[:, cols].astype(F32) * r)
            pup[:, cols] = r
    p_inv = pinv[:, 0:1]
    p_in = p_in * p_inv * p_inv
    for j in range(D // T):
        cols = slice(j * T, (j + 1) * T)
        gp_ref[:, cols] = ((pup[:, cols] - p_ref[:, cols].astype(F32) * p_in) * p_inv).astype(BF16)
    gp_out = pltpu.make_async_copy(gp_ref, gp_hbm, out_s.at[0])
    gp_out.start()

    back_p = dot(ab[16:32, :], gp_ref[...], NT).astype(BF16)
    arrive(yrcv.at[0:15], y_r, y_s)
    ysum = yrcv[0, :, 0:64]
    for s in range(1, 16):
        ysum = ysum + yrcv[s, :, 0:64]
    back = ((ysum - inner_row * ubt) * inv_row).astype(BF16)
    pick = lax.broadcasted_iota(I32, (64, 16), 0) == a * 16 + lax.broadcasted_iota(I32, (64, 16), 1)
    back_q = dot(back, pick.astype(F32).astype(BF16)).astype(BF16)
    back_all = jnp.concatenate([back_p, back_q], axis=1)
    low_all = jnp.concatenate([low_p, -low_q], axis=1)
    for j in range(D // T):
        cols = slice(j * T, (j + 1) * T)
        r = dot(back_all, jnp.concatenate([ap_ref[:, cols], aq_ref[:, cols]], axis=0))
        dsum[0:16, cols] = ADAPTER_SCALE * r
        v2 = (q_ref[:, cols].astype(F32) * (inner * q_inv * q_inv)).astype(BF16)
        r = dot(low_all, jnp.concatenate([gp_ref[:, cols], v2], axis=0))
        dsum[16:32, cols] = ADAPTER_SCALE * (dsum[16:32, cols] + r)
    mine = pl.ds(pl.multiple_of(core * 16, 16), 16)
    theirs = pl.ds(pl.multiple_of(other * 16, 16), 16)
    d_copy = push(dsum.at[theirs], dbuf, d_s, d_r, partner)

    shares(bp, 1, put_in(d1p, 1))
    shares(bm, 0, put_in(d1m, 0))
    shares(bp, 0, put_in(uf, 0))
    shares(bm, 1, put_in(uf, 1))

    arrive(dbuf, d_r, d_s)
    for j in range(D // 128):
        cols = slice(j * 128, (j + 1) * 128)
        drow[:, j // 2, j % 2, :] = dsum[mine, cols] + dbuf[:, cols]
    peers(lambda a_, b_, s: push(drow.at[s], rrow.at[me], rr_s, rr_r, at(a_, b_)))
    rrow[me] = drow[me]
    hop(2, d1p.at[1], r1m.at[1], at(a, bp))
    hop(3, d1m.at[0], r1p.at[0], at(a, bm))
    landed(rl1.at[0], 0)
    d1p[0] = (uf[0] + rl1[0].astype(F32)).astype(BF16)
    hop(4, d1p.at[0], r1m.at[0], at(a, bp))
    landed(rl1.at[1], 1)
    d1m[1] = (uf[1] + rl1[1].astype(F32)).astype(BF16)
    hop(5, d1m.at[1], r1p.at[1], at(a, bm))
    shares(b, 0, put_in(v1, 0))
    shares(b, 1, put_in(v1, 1))
    arrive(rrow.at[0:15], rr_r, rr_s)
    acc = rrow[0]
    for s in range(1, 16):
        acc = acc + rrow[s]
    zrow[...] = acc

    @pl.loop(0, 15)
    def _(k):
        zk = lax.rem(z + lax.rem(k + 4, 15) + 1, 16)
        push(zrow.at[zk], zbuf.at[z], z_s, z_r, (dp, zk))

    zbuf[z] = zrow[z]

    landed(r1m.at[1], 2)
    landed(r1p.at[0], 3)
    landed(r1m.at[0], 4)
    landed(r1p.at[1], 5)
    for h in range(2):
        v1[h] = v1[h] + r1m[h].astype(F32) + r1p[h].astype(F32)
        t2[h] = v1[h, a2].astype(BF16)
        if h == 0:
            hop(6, t2.at[0], rl2.at[0], at(ap, b))
            d2m[0] = v1[0, am].astype(BF16)
            hop(7, d2m.at[0], r2p.at[0], at(am, b))
        else:
            hop(8, t2.at[1], rl2.at[1], at(am, b))
            d2p[1] = v1[1, ap].astype(BF16)
            hop(9, d2p.at[1], r2m.at[1], at(ap, b))
    arrive(zbuf.at[0:15], z_r, z_s)
    acc = zbuf[0]
    for s in range(1, 16):
        acc = acc + zbuf[s]
    orow[...] = acc
    oall[core * 16 + me] = acc

    @pl.loop(1, 32)
    def _(k):
        push(orow, oall.at[core * 16 + me], o_s, o_r, (lax.rem(dp + k, 32), z))

    landed(rl2.at[0], 6)
    d2p[0] = (v1[0, ap] + rl2[0].astype(F32)).astype(BF16)
    hop(10, d2p.at[0], r2m.at[0], at(ap, b))
    landed(rl2.at[1], 8)
    d2m[1] = (v1[1, am] + rl2[1].astype(F32)).astype(BF16)
    hop(11, d2m.at[1], r2p.at[1], at(am, b))
    landed(r2p.at[0], 7)
    landed(r2m.at[1], 9)
    landed(r2m.at[0], 10)
    landed(r2p.at[1], 11)
    qu = jnp.concatenate(
        [v1[h, a] + r2m[h].astype(F32) + r2p[h].astype(F32) for h in range(2)], axis=1
    )
    qv = q_ref[...].astype(F32)
    q_inv = 1.0 / jnp.sqrt(lanes_sum(qv * qv) + EPSILON)
    q_in = lanes_sum(qv * qu) * q_inv * q_inv
    gq_ref[...] = ((qu - qv * q_in) * q_inv).astype(BF16)
    gq_out = pltpu.make_async_copy(gq_ref, gq_hbm, out_s.at[1])
    gq_out.start()

    for c in rs + [p_copy, d_copy, w_copy]:
        c.wait_send()
    gone(qown.at[0:15], ag_s.at[0], q_r.at[0, 0])
    gone(qown, ag_s.at[1], qo_r)
    gone(ab.at[:, 0 : 15 * 256], ab_s, ab_r)
    gone(csnd.at[0:15], c_s, c_r)
    gone(srcv.at[0:15], s_s, s_r)
    gone(grcv.at[0:15], g_s, g_r)
    gone(yrcv.at[0:15], y_s, y_r)
    gone(drow.at[0:15], rr_s, rr_r)
    gone(zrow.at[0:15], z_s, z_r)
    gone(oall.at[0:31], o_s, o_r)
    arrive(oall.at[0:31], o_r, o_s)
    outs = [gp_out, gq_out]
    for c_, dst in ((0, down_hbm), (1, up_hbm)):
        dv[c_, :, 0:128] = oall[c_ * 16 : c_ * 16 + 16, 0, :]
        dv[c_, :, 128:256] = oall[c_ * 16 : c_ * 16 + 16, 1, :]
        outs.append(pltpu.make_async_copy(dv.at[c_], dst, out_s.at[2 + c_]))
        outs[-1].start()

    for c in outs:
        c.wait()


def hand_over(*refs):
    copies = [pltpu.make_async_copy(refs[i], refs[4 + i], refs[8].at[i]) for i in (1, 0, 2, 3)]
    for c in copies:
        c.start()
    for c in copies:
        c.wait()


ANY = pl.BlockSpec(memory_space=pl.ANY)


def per_device(query, passage, query_attn, passage_attn, positives, negatives, home, down, up):
    dma = pltpu.SemaphoreType.DMA
    vm = pltpu.VMEM
    half = vm((2, 4, 16, H), BF16)
    row = vm((2, 16, H), BF16)
    grad_q, grad_p, sum_down, sum_up = pl.pallas_call(
        kernel,
        out_shape=(
            jax.ShapeDtypeStruct((16, D), BF16),
            jax.ShapeDtypeStruct((128, D), BF16),
            jax.ShapeDtypeStruct((16, 256), F32),
            jax.ShapeDtypeStruct((16, 256), F32),
        ),
        in_specs=[pl.BlockSpec(memory_space=pltpu.HBM)] * 9,
        out_specs=(ANY,) * 4,
        scratch_shapes=[
            vm((16, D), BF16),
            vm((128, D), BF16),
            vm((16, D), BF16),
            vm((128, D), BF16),
            vm((16, 64), I32),
            vm((32, 128), I32),
            vm((16, 256), BF16),
            vm((16, 256), BF16),
            pltpu.SMEM((1, 16), I32),
            vm((16, D), BF16),
            vm((128, D), BF16),
            vm((2, 16, 256), F32),
            vm((16, 2, 16, H), BF16),
            vm((16, 2, 16, H), BF16),
            vm((256, D), BF16),
            vm((32, D), BF16),
            vm((16, 128), I32),
            vm((256, H), BF16),
            vm((256, H), BF16),
            vm((16, 2, 16, 128), BF16),
            vm((16, 2, 16, 128), BF16),
            vm((4, 256, 64), F32),
            vm((4, 256, 64), F32),
            vm((4, 4, 128), F32),
            vm((16, 4, 4, 128), F32),
            vm((4, 4, 128), F32),
            vm((2, 256, 256), BF16),
            vm((2, 128, 256), BF16),
            vm((2, 256, 256), BF16),
            vm((16, 128), BF16),
            vm((16, 16, 128), BF16),
            vm((4, 16, 128), F32),
            vm((16, 16, 128), F32),
            half,
            half,
            half,
            half,
            half,
            half,
            vm((2, 4, 16, H), F32),
            vm((2, 4, 16, H), F32),
            row,
            row,
            row,
            row,
            row,
            row,
            vm((128, 128), F32),
            vm((128, D), F32),
            vm((32, D), F32),
            vm((16, D), F32),
            vm((16, 16, 2, 128), F32),
            vm((16, 16, 2, 128), F32),
            vm((16, 2, 128), F32),
            vm((16, 2, 128), F32),
            vm((2, 128), F32),
            vm((32, 2, 128), F32),
            dma((9,)),
            dma((4,)),
            dma((2,)),
            dma((16, 2)),
            dma(()),
            dma(()),
            dma(()),
            dma(()),
            dma(()),
            dma(()),
            dma(()),
            dma(()),
            dma(()),
            dma(()),
            dma(()),
            dma(()),
            dma(()),
            dma(()),
            dma(()),
            dma((12,)),
            dma((12,)),
            dma(()),
            dma(()),
            dma(()),
            dma(()),
            dma(()),
            dma(()),
            dma(()),
            dma(()),
        ],
        compiler_params=pltpu.CompilerParams(
            collective_id=0, has_side_effects=True, vmem_limit_bytes=26 * 1024 * 1024
        ),
    )(
        *(
            pltpu.with_memory_space_constraint(v, pltpu.HBM)
            for v in (
                query[0], passage[0], query_attn[0], passage_attn[0], negatives[0],
                home[0].reshape(32, 128), down, up, positives,
            )
        )
    )
    outs = pl.pallas_call(
        hand_over,
        out_shape=tuple(jax.ShapeDtypeStruct(v.shape, v.dtype) for v in (grad_q, grad_p, sum_down, sum_up)),
        in_specs=[ANY] * 4,
        out_specs=(ANY,) * 4,
        scratch_shapes=[dma((4,))],
        compiler_params=pltpu.CompilerParams(vmem_limit_bytes=1024 * 1024),
    )(grad_q, grad_p, sum_down, sum_up)
    return outs[0][None], outs[1][None], outs[2], outs[3]


def solution(mesh):
    in_specs = (
        P("fsdp", "dp", None),
        P("fsdp", "dp", None),
        P("fsdp", "dp", None),
        P("fsdp", "dp", None),
        P("fsdp", "dp"),
        P("fsdp", "dp", None),
        P("fsdp", None),
        P(None, "fsdp"),
        P(None, "fsdp"),
    )
    out_specs = (P("fsdp", "dp", None), P("fsdp", "dp", None), P(None, "fsdp"), P(None, "fsdp"))
    return jax.shard_map(
        per_device, mesh=mesh, in_specs=in_specs, out_specs=out_specs, check_vma=False
    )
```

```python
import jax
import jax.numpy as jnp
from jax import lax
from jax.experimental import pallas as pl
from jax.experimental.pallas import tpu as pltpu
from jax.sharding import PartitionSpec as P

MESH = pl.DeviceIdType.MESH
F32, BF16, I32 = jnp.float32, jnp.bfloat16, jnp.int32
HEAT = 100.0
ADAPTER_SCALE = 2.0
EPSILON = 1e-06
D = 4096
H = 2048
T = 512
NN = (((1,), (0,)), ((), ()))
NT = (((1,), (1,)), ((), ()))


def dot(lhs, rhs, dims=NN):
    return lax.dot_general(lhs, rhs, dims, preferred_element_type=F32)


def hi_lo(w):
    hi = w.astype(BF16)
    return hi, (w - hi.astype(F32)).astype(BF16)


def lanes_sum(v):
    return jnp.sum(v, axis=-1, keepdims=True)


def kernel(
    q_hbm, p_hbm, aq_hbm, ap_hbm, neg_hbm, home_hbm, aw_hbm, bw_hbm, pos_hbm,
    gq_hbm, gp_hbm, down_hbm, up_hbm,
    q_ref, p_ref, aq_ref, ap_ref, neg_ref, home_ref, aw_ref, bw_ref, pos_ref, gq_ref, gp_ref, dv,
    qown, qoth, pb, ab, negp, lhs, rhs, csnd, crcv, ct, est, stat, srcv, rows_s,
    wt, woth, wq, gsnd, grcv, ysnd, yrcv,
    t1, rl1, d1p, d1m, r1m, r1p, uf, v1, t2, rl2, d2p, d2m, r2m, r2p,
    pinv, pup, dsum, dbuf, drow, rrow, zrow, zbuf, orow, oall,
    in_s, out_s, ag_s, q_r, qo_r, p_s, p_r, ab_s, ab_r, abp_s, abp_r, near_s, c_s, c_r, s_s, s_r, w_s, w_r, g_s, g_r, y_s, y_r,
    rs_s, rs_r, d_s, d_r, rr_s, rr_r, z_s, z_r, o_s, o_r,
):
    dp, z = lax.axis_index("dp"), lax.axis_index("fsdp")
    core, chip = lax.rem(dp, 2), dp // 2
    x, y = chip // 4, lax.rem(chip, 4)
    a = x * (1 - core) + y * core
    b = y * (1 - core) + x * core
    sa, sb = 8 - 6 * core, 2 + 6 * core
    other = 1 - core

    def near(v, k):
        return lax.rem(v + k, 4)

    def at(a_, b_):
        return (a_ * sa + b_ * sb + core, z)

    def slot(a_, b_):
        return b_ * 4 + a_

    me = slot(a, b)
    partner = (chip * 2 + other, z)
    am, a2, ap = near(a, 3), near(a, 2), near(a, 1)
    bm, b2, bp = near(b, 3), near(b, 2), near(b, 1)

    barrier = pltpu.get_barrier_semaphore()

    loads = [
        pltpu.make_async_copy(src, dst, in_s.at[i])
        for i, (src, dst) in enumerate(
            (
                (q_hbm, q_ref), (p_hbm, p_ref), (aw_hbm, aw_ref), (bw_hbm, bw_ref),
                (neg_hbm, neg_ref), (home_hbm, home_ref), (aq_hbm, aq_ref), (ap_hbm, ap_ref), (pos_hbm, pos_ref),
            )
        )
    ]
    loads[0].start()
    loads[1].start()

    def tell_plane(sem):
        for device in (at(ap, b), at(am, b), at(a, bp), at(a, bm)):
            pl.semaphore_signal(sem, inc=1, device_id=device, device_id_type=MESH)

    pl.semaphore_signal(barrier, inc=1, device_id=partner, device_id_type=MESH)
    tell_plane(barrier)

    def tell_z(sem, step):
        for k in (step, 16 - step):
            pl.semaphore_signal(sem, inc=1, device_id=(dp, lax.rem(z + k, 16)), device_id_type=MESH)

    tell_z(barrier, 1)

    for c in loads[2:]:
        c.start()

    loads[0].wait()
    qv = q_ref[...].astype(F32)
    q_inv = 1.0 / jnp.sqrt(lanes_sum(qv * qv) + EPSILON)
    qe = (qv * q_inv).astype(BF16)
    qown[me, 0] = qe[:, :H]
    qown[me, 1] = qe[:, H:]
    for i in (2, 3):
        loads[i].wait()
    zcols = pl.ds(pl.multiple_of(z * 256, 256), 256)
    kind = pl.ds(pl.multiple_of(core * 16, 16), 16)
    other_kind = pl.ds(pl.multiple_of(other * 16, 16), 16)
    ab[kind, zcols] = jnp.where(core == 0, aw_ref[...], bw_ref[...])
    loads[1].wait()

    def p_rows(i, carry):
        rows = pl.ds(pl.multiple_of(i * 32, 32), 32)
        pv = p_ref[rows, :].astype(F32)
        inv = 1.0 / jnp.sqrt(lanes_sum(pv * pv) + EPSILON)
        pinv[rows, :] = jnp.broadcast_to(inv, (32, 128))
        dst = pl.ds(pl.multiple_of(core * 128 + i * 32, 32), 32)
        pb[dst, :] = (pv * inv).astype(BF16)
        return carry

    lax.fori_loop(0, 4, p_rows, 0)

    pl.semaphore_wait(barrier, 7)
    tell_z(near_s.at[0], 1)
    tell_plane(near_s.at[3])

    def push(src, dst, ssem, rsem, device):
        c = pltpu.make_async_remote_copy(
            src_ref=src, dst_ref=dst, send_sem=ssem, recv_sem=rsem, device_id=device, device_id_type=MESH
        )
        c.start()
        return c

    def arrive(dst, rsem, ssem):
        pltpu.make_async_remote_copy(
            src_ref=dst, dst_ref=dst, send_sem=ssem, recv_sem=rsem, device_id=partner, device_id_type=MESH
        ).wait_recv()

    def gone(src, ssem, rsem):
        pltpu.make_async_remote_copy(
            src_ref=src, dst_ref=src, send_sem=ssem, recv_sem=rsem, device_id=partner, device_id_type=MESH
        ).wait_send()

    def peers(body):
        def one(k):
            a_, b_ = near(a, lax.rem(6 - lax.rem(k, 4), 4)), near(b, lax.rem(6 - k // 4, 4))
            body(a_, b_, slot(a_, b_))

        pl.loop(0, 10)(one)
        pl.loop(11, 16)(one)

    def q_half(s, h, device):
        push(qown.at[s, h], qown.at[s, h], ag_s.at[0], q_r.at[s, h], device)

    def q_other(s):
        push(qown.at[s], qoth.at[s], ag_s.at[1], qo_r, partner)

    def got_half(s, h):
        arrive(qown.at[s, h], q_r.at[s, h], ag_s.at[0])

    q_half(me, 0, at(ap, b))
    q_half(me, 1, at(am, b))
    q_half(me, 1, at(ap, b))
    q_half(me, 0, at(am, b))
    own_rows = pl.ds(pl.multiple_of(core * 128, 128), 128)
    other_rows = pl.ds(pl.multiple_of(other * 128, 128), 128)
    p_copy = push(pb.at[own_rows], pb.at[own_rows], p_s, p_r, partner)
    q_other(me)

    loads[4].wait()
    loads[5].wait()
    loads[8].wait()
    negp[...] = jnp.full((16, 128), -1, I32)
    negp[:, 0:64] = neg_ref[...]
    n_row = jnp.concatenate([negp[k : k + 1, :] for k in range(16)], axis=1)
    home = home_ref[...]
    table = jnp.concatenate(
        [(home >> 7).astype(F32).T, (home & 127).astype(F32).T], axis=0
    ).astype(BF16)
    for part in range(4):
        if part == 1:
            q_half(me, 0, at(a, bp))
            q_half(me, 1, at(a, bm))
            q_half(me, 1, at(a, bp))
            q_half(me, 0, at(a, bm))
        n = n_row[:, part * T : (part + 1) * T]
        lane_q = (lax.broadcasted_iota(I32, (1, T), 1) >> 7) + part * 4
        picked = (lax.broadcasted_iota(I32, (32, T), 0) == (n >> 7)).astype(F32).astype(BF16)
        found = dot(table, picked)
        low = lax.broadcasted_iota(I32, (128, T), 0) == (n & 127)
        dev_row = jnp.sum(jnp.where(low, found[0:128], 0.0), axis=0, keepdims=True).astype(I32)
        in_dev = jnp.sum(jnp.where(low, found[128:256], 0.0), axis=0, keepdims=True).astype(I32)
        chip_row = dev_row >> 1
        key = ((chip_row >> 2) * (1 + 3 * core) + (chip_row & 3) * (4 - 3 * core)) * 16 + lane_q
        key = jnp.where(n >= 0, key, -1)
        col = (dev_row & 1) * 128 + in_dev
        rows = lax.broadcasted_iota(I32, (256, T), 0)
        lhs[:, part * T : (part + 1) * T] = (rows == key).astype(F32).astype(BF16)
        rhs[:, part * T : (part + 1) * T] = (rows == col).astype(F32).astype(BF16)
    times = dot(lhs[...], rhs[...], NT).astype(BF16)
    csnd[:, 0] = times[:, 0:128].reshape(16, 16, 128)
    csnd[:, 1] = times[:, 128:256].reshape(16, 16, 128)
    crcv[me] = csnd[me]
    lane = lax.broadcasted_iota(I32, (1, 64), 1)
    pos_row = jnp.full((1, 64), -1000, I32)
    for k in range(16):
        pos_row = jnp.where(lane == a * 16 + k, pos_ref[0, k], pos_row)
    pos_hot = (lax.broadcasted_iota(I32, (256, 64), 0) == pos_row + core * 128).astype(F32)
    own_lane = lax.broadcasted_iota(I32, (16, 64), 1) == a * 16 + lax.broadcasted_iota(I32, (16, 64), 0)

    def counts_ready():
        arrive(crcv.at[0:15], c_r, c_s)
        for i in range(4):
            for k in range(2):
                ct[i, k * 128 : (k + 1) * 128, :] = (
                    crcv[i * 4 : i * 4 + 4, k].astype(F32).reshape(64, 128).T
                )
        ct[b] = ct[b] + pos_hot

    def scores(*blocks):
        def rows_of(h):
            got = [qown[pl.ds(b_ * 4, 4), h].reshape(64, H) for b_ in blocks]
            return got[0] if len(got) == 1 else jnp.concatenate(got, axis=0)

        s = dot(pb[:, 0:H], rows_of(0), NT)
        s = (s + dot(pb[:, H:D], rows_of(1), NT)) * HEAT
        return [s[:, i * 64 : (i + 1) * 64] for i in range(len(blocks))]

    def statistics(b_, s):
        c = ct[b_]
        named = c > 0.0
        top = jnp.max(jnp.where(named, s, -1e30), axis=0, keepdims=True)
        e = c * jnp.exp(jnp.where(named, s - top, -1e30))
        est[b_] = e
        side = (lax.broadcasted_iota(I32, (1, 128), 1) >> 6) == lax.rem(b_, 2)
        sums = (top, jnp.sum(e, axis=0, keepdims=True), jnp.sum(e * s, axis=0, keepdims=True))
        for k, v in enumerate(sums):
            row = stat[b_ // 2, k : k + 1, :]
            stat[b_ // 2, k : k + 1, :] = jnp.where(side, jnp.concatenate([v, v], axis=1), row)

    pl.semaphore_wait(near_s.at[0], 2)
    tell_z(near_s.at[1], 2)
    pl.semaphore_wait(near_s.at[3], 4)
    tell_plane(near_s.at[4])
    got_half(slot(am, b), 0)
    q_half(slot(am, b), 0, at(ap, b))
    q_half(slot(am, b), 0, at(a, bp))
    got_half(slot(ap, b), 1)
    q_half(slot(ap, b), 1, at(am, b))
    q_half(slot(ap, b), 1, at(a, bm))
    pl.semaphore_wait(near_s.at[4], 4)
    tell_plane(near_s.at[5])
    got_half(slot(am, b), 1)
    q_half(slot(am, b), 1, at(a, bm))
    q_half(slot(am, b), 1, at(a, bp))
    got_half(slot(ap, b), 0)
    q_half(slot(ap, b), 0, at(a, bp))
    q_half(slot(ap, b), 0, at(a, bm))
    q_half(slot(am, b), 0, at(a, bm))
    q_half(slot(ap, b), 1, at(a, bp))
    q_other(slot(am, b))
    q_other(slot(ap, b))
    pl.semaphore_wait(near_s.at[1], 2)
    tell_z(near_s.at[2], 4)
    pl.semaphore_wait(near_s.at[5], 4)
    peers(lambda a_, b_, s: push(csnd.at[s], crcv.at[me], c_s, c_r, at(a_, b_)))
    got_half(slot(a2, b), 0)
    q_half(slot(a2, b), 0, at(a, bp))
    got_half(slot(a2, b), 1)
    q_half(slot(a2, b), 1, at(a, bm))
    q_half(slot(a2, b), 1, at(a, bp))
    q_half(slot(a2, b), 0, at(a, bm))
    q_other(slot(a2, b))
    got_half(slot(a, bm), 0)
    q_half(slot(a, bm), 0, at(a, bp))
    got_half(slot(a, bp), 1)
    q_half(slot(a, bp), 1, at(a, bm))
    pl.semaphore_wait(near_s.at[2], 2)

    @pl.loop(0, 15)
    def _(k):
        zk = lax.rem(z + lax.rem(k + 5, 15) + 1, 16)
        push(ab.at[kind, zcols], ab.at[kind, zcols], ab_s, ab_r, (dp, zk))

    arrive(pb.at[other_rows], p_r, p_s)
    (s_b,) = scores(b)
    for a_ in (am, ap):
        got_half(slot(a_, bm), 0)
        q_half(slot(a_, bm), 0, at(a, bp))
        got_half(slot(a_, bp), 1)
        q_half(slot(a_, bp), 1, at(a, bm))
    got_half(slot(a2, bm), 0)
    q_half(slot(a2, bm), 0, at(a, bp))
    got_half(slot(a2, bp), 1)
    q_half(slot(a2, bp), 1, at(a, bm))
    for a_ in (a, am, ap, a2):
        got_half(slot(a_, bm), 1)
        got_half(slot(a_, bp), 0)
        q_other(slot(a_, bm))
        q_other(slot(a_, bp))
    s_m, s_p = scores(bm, bp)
    counts_ready()
    s_pos = jnp.sum(pos_hot * s_b, axis=0, keepdims=True)
    statistics(b, s_b)
    statistics(bm, s_m)
    statistics(bp, s_p)
    for a_ in (a, am, ap, a2):
        for h in range(2):
            got_half(slot(a_, b2), h)
    (s_2,) = scores(b2)
    statistics(b2, s_2)
    peers(lambda a_, b_, s: push(stat, srcv.at[me], s_s, s_r, at(a_, b_)))
    srcv[me] = stat[...]
    for a_ in (a, am, ap, a2):
        q_other(slot(a_, b2))

    arrive(ab.at[kind, 0 : 15 * 256], ab_r, ab_s)
    ab_copy = push(ab.at[kind, :], ab.at[kind, :], abp_s, abp_r, partner)
    arrive(ab.at[other_kind, :], abp_r, abp_s)
    loads[6].wait()
    loads[7].wait()
    low_rows = dot(aq_ref[...], ab[0:16, :], NT).astype(BF16).astype(F32) * q_inv
    g_hi, g_lo = hi_lo(low_rows)
    gsnd[...] = jnp.zeros((16, 128), BF16)
    gsnd[:, 0:16] = g_hi
    gsnd[:, 16:32] = g_lo
    grcv[me] = gsnd[...]
    peers(lambda a_, b_, s: push(gsnd, grcv.at[me], g_s, g_r, at(a_, b_)))
    low_p = dot(ab[0:16, :], ap_ref[...], NT).astype(BF16)
    low_q = dot(ab[0:16, :], aq_ref[...], NT).astype(BF16)
    pbt = jnp.concatenate(hi_lo(dot(ab[16:32, :], pb[...], NT)), axis=0)
    block = pl.ds(b * 4, 4)
    ubt = dot(ab[16:32, 0:H], qown[block, 0].reshape(64, H), NT)
    ubt = ubt + dot(ab[16:32, H:D], qown[block, 1].reshape(64, H), NT)
    inv_row = jnp.sum(jnp.where(own_lane, q_inv, 0.0), axis=0, keepdims=True)

    arrive(srcv.at[0:15], s_r, s_s)

    top = srcv[0, :, 0:1, :]
    for s in range(1, 16):
        top = jnp.maximum(top, srcv[s, :, 0:1, :])
    total = jnp.zeros((2, 1, 128), F32)
    first = jnp.zeros((2, 1, 128), F32)
    for s in range(16):
        f = jnp.exp(srcv[s, :, 0:1, :] - top)
        total = total + f * srcv[s, :, 1:2, :]
        first = first + f * srcv[s, :, 2:3, :]
    rows_s[:, 0:1, :] = jnp.exp(stat[:, 0:1, :] - top) * (HEAT / total)
    rows_s[:, 1:2, :] = first / total
    for i in range(4):
        est[i] = est[i] * rows_s[i // 2, 0:1, i % 2 * 64 : i % 2 * 64 + 64]
    est[b] = est[b] - HEAT * pos_hot
    weight = jnp.concatenate([est[i] for i in range(4)], axis=1)
    w_hi, w_lo = hi_lo(weight)
    wt[0] = w_hi
    wt[1] = w_lo
    w_copy = push(wt.at[:, other_rows], woth, w_s, w_r, partner)
    mean = rows_s[b // 2, 1:2, :]
    inner_row = jnp.where(lax.rem(b, 2) == 0, mean[:, 0:64], mean[:, 64:128]) - s_pos
    inner = lanes_sum(jnp.where(own_lane, inner_row, 0.0))

    share = dot(pbt, w_hi) + dot(pbt, w_lo)
    share = share[0:16] + share[16:32]
    for i in range(4):
        ysnd[i, :, 0:64] = share[:, i * 64 : (i + 1) * 64]
    peers(lambda a_, b_, s: push(ysnd.at[b_], yrcv.at[me], y_s, y_r, at(a_, b_)))
    yrcv[me] = ysnd[b]
    arrive(grcv.at[0:15], g_r, g_s)
    gall = grcv[...].reshape(256, 128)
    xt = (dot(wt[0], gall) + dot(wt[1], gall)).T
    xs = jnp.concatenate(hi_lo(xt[0:16] + xt[16:32]), axis=0)

    wq_hi, wq_lo = hi_lo(weight.T)
    wq[0] = wq_hi
    wq[1] = wq_lo

    def shares(b_, h, put):
        rows = pl.ds(pl.multiple_of(b_ * 64, 64), 64)
        w = jnp.concatenate([wq[0, rows, :], wq[1, rows, :]], axis=0)
        for j in range(H // T):
            r = dot(w, pb[:, h * H + j * T : h * H + (j + 1) * T])
            put(slice(j * T, (j + 1) * T), (r[0:64] + r[64:128]).reshape(4, 16, T))

    def put_in(ref, *where):
        def put(cols, r):
            ref[(*where, slice(None), slice(None), cols)] = r.astype(ref.dtype)

        return put

    rs = []

    def hop(n, src, dst, device):
        rs.append(push(src, dst, rs_s.at[n], rs_r.at[n], device))

    def landed(dst, n):
        arrive(dst, rs_r.at[n], rs_s.at[0])

    shares(b2, 0, put_in(t1, 0))
    hop(0, t1.at[0], rl1.at[0], at(a, bp))
    shares(b2, 1, put_in(t1, 1))
    hop(1, t1.at[1], rl1.at[1], at(a, bm))
    shares(bp, 1, put_in(d1p, 1))
    hop(2, d1p.at[1], r1m.at[1], at(a, bp))
    shares(bm, 0, put_in(d1m, 0))
    hop(3, d1m.at[0], r1p.at[0], at(a, bm))

    def two_parts(w, q, h, sub):
        r = dot(w, q[:, h, :, sub].reshape(256, T))
        return r[0:128] + r[128:256]

    wa = jnp.concatenate([wt[0, own_rows, :], wt[1, own_rows, :]], axis=0)
    for h in range(2):
        for j in range(H // T):
            cols = slice(h * H + j * T, h * H + (j + 1) * T)
            pup[:, cols] = two_parts(wa, qown, h, slice(j * T, (j + 1) * T))
            r = dot(xs, pb[:, cols])
            dsum[16:32, cols] = r[0:16] + r[16:32]
    arrive(qoth, qo_r, ag_s.at[1])
    arrive(woth, w_r, w_s)
    wb = jnp.concatenate([woth[0], woth[1]], axis=0)
    p_in = jnp.zeros((128, 1), F32)
    for h in range(2):
        for j in range(H // T):
            cols = slice(h * H + j * T, h * H + (j + 1) * T)
            r = pup[:, cols] + two_parts(wb, qoth, h, slice(j * T, (j + 1) * T))
            p_in = p_in + lanes_sum(p_ref[:, cols].astype(F32) * r)
            pup[:, cols] = r
    p_inv = pinv[:, 0:1]
    p_in = p_in * p_inv * p_inv
    for j in range(D // T):
        cols = slice(j * T, (j + 1) * T)
        gp_ref[:, cols] = ((pup[:, cols] - p_ref[:, cols].astype(F32) * p_in) * p_inv).astype(BF16)
    gp_out = pltpu.make_async_copy(gp_ref, gp_hbm, out_s.at[0])
    gp_out.start()

    back_p = dot(ab[16:32, :], gp_ref[...], NT).astype(BF16)
    arrive(yrcv.at[0:15], y_r, y_s)
    ysum = yrcv[0, :, 0:64]
    for s in range(1, 16):
        ysum = ysum + yrcv[s, :, 0:64]
    back = ((ysum - inner_row * ubt) * inv_row).astype(BF16)
    pick = lax.broadcasted_iota(I32, (64, 16), 0) == a * 16 + lax.broadcasted_iota(I32, (64, 16), 1)
    back_q = dot(back, pick.astype(F32).astype(BF16)).astype(BF16)
    back_all = jnp.concatenate([back_p, back_q], axis=1)
    low_all = jnp.concatenate([low_p, -low_q], axis=1)
    for j in range(D // T):
        cols = slice(j * T, (j + 1) * T)
        r = dot(back_all, jnp.concatenate([ap_ref[:, cols], aq_ref[:, cols]], axis=0))
        dsum[0:16, cols] = ADAPTER_SCALE * r
        v2 = (q_ref[:, cols].astype(F32) * (inner * q_inv * q_inv)).astype(BF16)
        r = dot(low_all, jnp.concatenate([gp_ref[:, cols], v2], axis=0))
        dsum[16:32, cols] = ADAPTER_SCALE * (dsum[16:32, cols] + r)
    mine = pl.ds(pl.multiple_of(core * 16, 16), 16)
    theirs = pl.ds(pl.multiple_of(other * 16, 16), 16)
    d_copy = push(dsum.at[theirs], dbuf, d_s, d_r, partner)

    shares(bp, 0, put_in(uf, 0))
    shares(bm, 1, put_in(uf, 1))

    arrive(dbuf, d_r, d_s)
    for j in range(D // 128):
        cols = slice(j * 128, (j + 1) * 128)
        drow[:, j // 2, j % 2, :] = dsum[mine, cols] + dbuf[:, cols]
    peers(lambda a_, b_, s: push(drow.at[s], rrow.at[me], rr_s, rr_r, at(a_, b_)))
    rrow[me] = drow[me]
    landed(rl1.at[0], 0)
    d1p[0] = (uf[0] + rl1[0].astype(F32)).astype(BF16)
    hop(4, d1p.at[0], r1m.at[0], at(a, bp))
    landed(rl1.at[1], 1)
    d1m[1] = (uf[1] + rl1[1].astype(F32)).astype(BF16)
    hop(5, d1m.at[1], r1p.at[1], at(a, bm))
    shares(b, 0, put_in(v1, 0))
    shares(b, 1, put_in(v1, 1))
    arrive(rrow.at[0:15], rr_r, rr_s)
    acc = rrow[0]
    for s in range(1, 16):
        acc = acc + rrow[s]
    zrow[...] = acc

    @pl.loop(0, 15)
    def _(k):
        zk = lax.rem(z + lax.rem(k + 4, 15) + 1, 16)
        push(zrow.at[zk], zbuf.at[z], z_s, z_r, (dp, zk))

    zbuf[z] = zrow[z]

    landed(r1m.at[1], 2)
    landed(r1p.at[0], 3)
    landed(r1m.at[0], 4)
    landed(r1p.at[1], 5)
    for h in range(2):
        v1[h] = v1[h] + r1m[h].astype(F32) + r1p[h].astype(F32)
        t2[h] = v1[h, a2].astype(BF16)
        if h == 0:
            hop(6, t2.at[0], rl2.at[0], at(ap, b))
            d2m[0] = v1[0, am].astype(BF16)
            hop(7, d2m.at[0], r2p.at[0], at(am, b))
        else:
            hop(8, t2.at[1], rl2.at[1], at(am, b))
            d2p[1] = v1[1, ap].astype(BF16)
            hop(9, d2p.at[1], r2m.at[1], at(ap, b))
    arrive(zbuf.at[0:15], z_r, z_s)
    acc = zbuf[0]
    for s in range(1, 16):
        acc = acc + zbuf[s]
    orow[...] = acc
    oall[core * 16 + me] = acc

    @pl.loop(1, 32)
    def _(k):
        push(orow, oall.at[core * 16 + me], o_s, o_r, (lax.rem(dp + k, 32), z))

    landed(rl2.at[0], 6)
    d2p[0] = (v1[0, ap] + rl2[0].astype(F32)).astype(BF16)
    hop(10, d2p.at[0], r2m.at[0], at(ap, b))
    landed(rl2.at[1], 8)
    d2m[1] = (v1[1, am] + rl2[1].astype(F32)).astype(BF16)
    hop(11, d2m.at[1], r2p.at[1], at(am, b))
    landed(r2p.at[0], 7)
    landed(r2m.at[1], 9)
    landed(r2m.at[0], 10)
    landed(r2p.at[1], 11)
    qu = jnp.concatenate(
        [v1[h, a] + r2m[h].astype(F32) + r2p[h].astype(F32) for h in range(2)], axis=1
    )
    qv = q_ref[...].astype(F32)
    q_inv = 1.0 / jnp.sqrt(lanes_sum(qv * qv) + EPSILON)
    q_in = lanes_sum(qv * qu) * q_inv * q_inv
    gq_ref[...] = ((qu - qv * q_in) * q_inv).astype(BF16)
    gq_out = pltpu.make_async_copy(gq_ref, gq_hbm, out_s.at[1])
    gq_out.start()

    for c in rs + [p_copy, d_copy, w_copy, ab_copy]:
        c.wait_send()
    gone(qown.at[0:15], ag_s.at[0], q_r.at[0, 0])
    gone(qown, ag_s.at[1], qo_r)
    gone(ab.at[kind, 0 : 15 * 256], ab_s, ab_r)
    gone(csnd.at[0:15], c_s, c_r)
    gone(srcv.at[0:15], s_s, s_r)
    gone(grcv.at[0:15], g_s, g_r)
    gone(yrcv.at[0:15], y_s, y_r)
    gone(drow.at[0:15], rr_s, rr_r)
    gone(zrow.at[0:15], z_s, z_r)
    gone(oall.at[0:31], o_s, o_r)
    arrive(oall.at[0:31], o_r, o_s)
    outs = [gp_out, gq_out]
    for c_, dst in ((0, down_hbm), (1, up_hbm)):
        dv[c_, :, 0:128] = oall[c_ * 16 : c_ * 16 + 16, 0, :]
        dv[c_, :, 128:256] = oall[c_ * 16 : c_ * 16 + 16, 1, :]
        outs.append(pltpu.make_async_copy(dv.at[c_], dst, out_s.at[2 + c_]))
        outs[-1].start()

    for c in outs:
        c.wait()


def hand_over(*refs):
    copies = [pltpu.make_async_copy(refs[i], refs[4 + i], refs[8].at[i]) for i in (1, 0, 2, 3)]
    for c in copies:
        c.start()
    for c in copies:
        c.wait()


ANY = pl.BlockSpec(memory_space=pl.ANY)


def per_device(query, passage, query_attn, passage_attn, positives, negatives, home, down, up):
    dma = pltpu.SemaphoreType.DMA
    vm = pltpu.VMEM
    half = vm((2, 4, 16, H), BF16)
    row = vm((2, 16, H), BF16)
    grad_q, grad_p, sum_down, sum_up = pl.pallas_call(
        kernel,
        out_shape=(
            jax.ShapeDtypeStruct((16, D), BF16),
            jax.ShapeDtypeStruct((128, D), BF16),
            jax.ShapeDtypeStruct((16, 256), F32),
            jax.ShapeDtypeStruct((16, 256), F32),
        ),
        in_specs=[pl.BlockSpec(memory_space=pltpu.HBM)] * 9,
        out_specs=(ANY,) * 4,
        scratch_shapes=[
            vm((16, D), BF16),
            vm((128, D), BF16),
            vm((16, D), BF16),
            vm((128, D), BF16),
            vm((16, 64), I32),
            vm((32, 128), I32),
            vm((16, 256), BF16),
            vm((16, 256), BF16),
            pltpu.SMEM((1, 16), I32),
            vm((16, D), BF16),
            vm((128, D), BF16),
            vm((2, 16, 256), F32),
            vm((16, 2, 16, H), BF16),
            vm((16, 2, 16, H), BF16),
            vm((256, D), BF16),
            vm((32, D), BF16),
            vm((16, 128), I32),
            vm((256, H), BF16),
            vm((256, H), BF16),
            vm((16, 2, 16, 128), BF16),
            vm((16, 2, 16, 128), BF16),
            vm((4, 256, 64), F32),
            vm((4, 256, 64), F32),
            vm((2, 4, 128), F32),
            vm((16, 2, 4, 128), F32),
            vm((2, 4, 128), F32),
            vm((2, 256, 256), BF16),
            vm((2, 128, 256), BF16),
            vm((2, 256, 256), BF16),
            vm((16, 128), BF16),
            vm((16, 16, 128), BF16),
            vm((4, 16, 128), F32),
            vm((16, 16, 128), F32),
            half,
            half,
            half,
            half,
            half,
            half,
            vm((2, 4, 16, H), F32),
            vm((2, 4, 16, H), F32),
            row,
            row,
            row,
            row,
            row,
            row,
            vm((128, 128), F32),
            vm((128, D), F32),
            vm((32, D), F32),
            vm((16, D), F32),
            vm((16, 16, 2, 128), F32),
            vm((16, 16, 2, 128), F32),
            vm((16, 2, 128), F32),
            vm((16, 2, 128), F32),
            vm((2, 128), F32),
            vm((32, 2, 128), F32),
            dma((9,)),
            dma((4,)),
            dma((2,)),
            dma((16, 2)),
            dma(()),
            dma(()),
            dma(()),
            dma(()),
            dma(()),
            dma(()),
            dma(()),
            pltpu.SemaphoreType.REGULAR((6,)),
            dma(()),
            dma(()),
            dma(()),
            dma(()),
            dma(()),
            dma(()),
            dma(()),
            dma(()),
            dma(()),
            dma(()),
            dma((12,)),
            dma((12,)),
            dma(()),
            dma(()),
            dma(()),
            dma(()),
            dma(()),
            dma(()),
            dma(()),
            dma(()),
        ],
        compiler_params=pltpu.CompilerParams(
            collective_id=0, has_side_effects=True, vmem_limit_bytes=26 * 1024 * 1024
        ),
    )(
        *(
            pltpu.with_memory_space_constraint(v, pltpu.HBM)
            for v in (
                query[0], passage[0], query_attn[0], passage_attn[0], negatives[0],
                home[0].reshape(32, 128), down, up, positives,
            )
        )
    )
    outs = pl.pallas_call(
        hand_over,
        out_shape=tuple(jax.ShapeDtypeStruct(v.shape, v.dtype) for v in (grad_q, grad_p, sum_down, sum_up)),
        in_specs=[ANY] * 4,
        out_specs=(ANY,) * 4,
        scratch_shapes=[dma((4,))],
        compiler_params=pltpu.CompilerParams(vmem_limit_bytes=1024 * 1024),
    )(grad_q, grad_p, sum_down, sum_up)
    return outs[0][None], outs[1][None], outs[2], outs[3]


def solution(mesh):
    in_specs = (
        P("fsdp", "dp", None),
        P("fsdp", "dp", None),
        P("fsdp", "dp", None),
        P("fsdp", "dp", None),
        P("fsdp", "dp"),
        P("fsdp", "dp", None),
        P("fsdp", None),
        P(None, "fsdp"),
        P(None, "fsdp"),
    )
    out_specs = (P("fsdp", "dp", None), P("fsdp", "dp", None), P(None, "fsdp"), P(None, "fsdp"))
    return jax.shard_map(
        per_device, mesh=mesh, in_specs=in_specs, out_specs=out_specs, check_vma=False
    )
```

```python
import jax
import jax.numpy as jnp
from jax import lax
from jax.experimental import pallas as pl
from jax.experimental.pallas import tpu as pltpu
from jax.sharding import PartitionSpec as P

MESH = pl.DeviceIdType.MESH
F32, BF16, I32 = jnp.float32, jnp.bfloat16, jnp.int32
HEAT = 100.0
ADAPTER_SCALE = 2.0
EPSILON = 1e-06
D = 4096
H = 2048
T = 512
NN = (((1,), (0,)), ((), ()))
NT = (((1,), (1,)), ((), ()))


def dot(lhs, rhs, dims=NN):
    return lax.dot_general(lhs, rhs, dims, preferred_element_type=F32)


def hi_lo(w):
    hi = w.astype(BF16)
    return hi, (w - hi.astype(F32)).astype(BF16)


def lanes_sum(v):
    return jnp.sum(v, axis=-1, keepdims=True)


def kernel(
    q_hbm, p_hbm, aq_hbm, ap_hbm, neg_hbm, home_hbm, aw_hbm, bw_hbm, pos_hbm,
    gq_hbm, gp_hbm, down_hbm, up_hbm,
    q_ref, p_ref, aq_ref, ap_ref, neg_ref, home_ref, aw_ref, bw_ref, pos_ref, gq_ref, gp_ref, dv,
    qown, qoth, pb, ab, negp, lhs, rhs, csnd, crcv, ct, est, stat, srcv, rows_s,
    wt, woth, wq, gsnd, grcv, ysnd, yrcv,
    t1, rl1, d1p, d1m, r1m, r1p, uf, v1, t2, rl2, d2p, d2m, r2m, r2p,
    pinv, pup, dsum, dbuf, drow, rrow, zrow, zbuf, orow, oall,
    in_s, out_s, ag_s, q_r, qo_r, p_s, p_r, ab_s, ab_r, abp_s, abp_r, near_s, c_s, c_r, s_s, s_r, w_s, w_r, g_s, g_r, y_s, y_r,
    rs_s, rs_r, d_s, d_r, rr_s, rr_r, z_s, z_r, o_s, o_r,
):
    dp, z = lax.axis_index("dp"), lax.axis_index("fsdp")
    core, chip = lax.rem(dp, 2), dp // 2
    x, y = chip // 4, lax.rem(chip, 4)
    a = x * (1 - core) + y * core
    b = y * (1 - core) + x * core
    sa, sb = 8 - 6 * core, 2 + 6 * core
    other = 1 - core

    def near(v, k):
        return lax.rem(v + k, 4)

    def at(a_, b_):
        return (a_ * sa + b_ * sb + core, z)

    def slot(a_, b_):
        return b_ * 4 + a_

    me = slot(a, b)
    partner = (chip * 2 + other, z)
    am, a2, ap = near(a, 3), near(a, 2), near(a, 1)
    bm, b2, bp = near(b, 3), near(b, 2), near(b, 1)

    barrier = pltpu.get_barrier_semaphore()

    loads = [
        pltpu.make_async_copy(src, dst, in_s.at[i])
        for i, (src, dst) in enumerate(
            (
                (q_hbm, q_ref), (p_hbm, p_ref), (aw_hbm, aw_ref), (bw_hbm, bw_ref),
                (neg_hbm, neg_ref), (home_hbm, home_ref), (aq_hbm, aq_ref), (ap_hbm, ap_ref), (pos_hbm, pos_ref),
            )
        )
    ]
    loads[0].start()
    loads[1].start()

    def tell_plane(sem):
        for device in (at(ap, b), at(am, b), at(a, bp), at(a, bm)):
            pl.semaphore_signal(sem, inc=1, device_id=device, device_id_type=MESH)

    pl.semaphore_signal(barrier, inc=1, device_id=partner, device_id_type=MESH)
    tell_plane(barrier)

    def tell_z(sem, step):
        for k in (step, 16 - step):
            pl.semaphore_signal(sem, inc=1, device_id=(dp, lax.rem(z + k, 16)), device_id_type=MESH)

    tell_z(barrier, 1)

    for c in loads[2:]:
        c.start()

    loads[0].wait()
    qv = q_ref[...].astype(F32)
    q_inv = 1.0 / jnp.sqrt(lanes_sum(qv * qv) + EPSILON)
    qe = (qv * q_inv).astype(BF16)
    qown[me, 0] = qe[:, :H]
    qown[me, 1] = qe[:, H:]
    pl.semaphore_wait(barrier, 7)
    tell_z(near_s.at[0], 1)
    tell_plane(near_s.at[3])

    def push(src, dst, ssem, rsem, device):
        c = pltpu.make_async_remote_copy(
            src_ref=src, dst_ref=dst, send_sem=ssem, recv_sem=rsem, device_id=device, device_id_type=MESH
        )
        c.start()
        return c

    def arrive(dst, rsem, ssem):
        pltpu.make_async_remote_copy(
            src_ref=dst, dst_ref=dst, send_sem=ssem, recv_sem=rsem, device_id=partner, device_id_type=MESH
        ).wait_recv()

    def gone(src, ssem, rsem):
        pltpu.make_async_remote_copy(
            src_ref=src, dst_ref=src, send_sem=ssem, recv_sem=rsem, device_id=partner, device_id_type=MESH
        ).wait_send()

    def peers(body):
        def one(k):
            a_, b_ = near(a, lax.rem(6 - lax.rem(k, 4), 4)), near(b, lax.rem(6 - k // 4, 4))
            body(a_, b_, slot(a_, b_))

        pl.loop(0, 10)(one)
        pl.loop(11, 16)(one)

    def q_half(s, h, device):
        push(qown.at[s, h], qown.at[s, h], ag_s.at[0], q_r.at[s, h], device)

    def q_other(s):
        push(qown.at[s], qoth.at[s], ag_s.at[1], qo_r, partner)

    def got_half(s, h):
        arrive(qown.at[s, h], q_r.at[s, h], ag_s.at[0])

    q_half(me, 0, at(ap, b))
    q_half(me, 1, at(am, b))
    q_half(me, 1, at(ap, b))
    q_half(me, 0, at(am, b))
    for i in (2, 3):
        loads[i].wait()
    zcols = pl.ds(pl.multiple_of(z * 256, 256), 256)
    kind = pl.ds(pl.multiple_of(core * 16, 16), 16)
    other_kind = pl.ds(pl.multiple_of(other * 16, 16), 16)
    ab[kind, zcols] = jnp.where(core == 0, aw_ref[...], bw_ref[...])
    loads[1].wait()

    def p_rows(i, carry):
        rows = pl.ds(pl.multiple_of(i * 32, 32), 32)
        pv = p_ref[rows, :].astype(F32)
        inv = 1.0 / jnp.sqrt(lanes_sum(pv * pv) + EPSILON)
        pinv[rows, :] = jnp.broadcast_to(inv, (32, 128))
        dst = pl.ds(pl.multiple_of(core * 128 + i * 32, 32), 32)
        pb[dst, :] = (pv * inv).astype(BF16)
        return carry

    lax.fori_loop(0, 4, p_rows, 0)
    own_rows = pl.ds(pl.multiple_of(core * 128, 128), 128)
    other_rows = pl.ds(pl.multiple_of(other * 128, 128), 128)
    p_copy = push(pb.at[own_rows], pb.at[own_rows], p_s, p_r, partner)
    q_other(me)

    q_half(me, 0, at(a, bp))
    q_half(me, 1, at(a, bm))
    q_half(me, 1, at(a, bp))
    q_half(me, 0, at(a, bm))

    loads[4].wait()
    loads[5].wait()
    loads[8].wait()
    negp[...] = jnp.full((16, 128), -1, I32)
    negp[:, 0:64] = neg_ref[...]
    n_row = jnp.concatenate([negp[k : k + 1, :] for k in range(16)], axis=1)
    home = home_ref[...]
    table = jnp.concatenate(
        [(home >> 7).astype(F32).T, (home & 127).astype(F32).T], axis=0
    ).astype(BF16)
    for part in range(4):
        n = n_row[:, part * T : (part + 1) * T]
        lane_q = (lax.broadcasted_iota(I32, (1, T), 1) >> 7) + part * 4
        picked = (lax.broadcasted_iota(I32, (32, T), 0) == (n >> 7)).astype(F32).astype(BF16)
        found = dot(table, picked)
        low = lax.broadcasted_iota(I32, (128, T), 0) == (n & 127)
        dev_row = jnp.sum(jnp.where(low, found[0:128], 0.0), axis=0, keepdims=True).astype(I32)
        in_dev = jnp.sum(jnp.where(low, found[128:256], 0.0), axis=0, keepdims=True).astype(I32)
        chip_row = dev_row >> 1
        key = ((chip_row >> 2) * (1 + 3 * core) + (chip_row & 3) * (4 - 3 * core)) * 16 + lane_q
        key = jnp.where(n >= 0, key, -1)
        col = (dev_row & 1) * 128 + in_dev
        rows = lax.broadcasted_iota(I32, (256, T), 0)
        lhs[:, part * T : (part + 1) * T] = (rows == key).astype(F32).astype(BF16)
        rhs[:, part * T : (part + 1) * T] = (rows == col).astype(F32).astype(BF16)
    times = dot(lhs[...], rhs[...], NT).astype(BF16)
    csnd[:, 0] = times[:, 0:128].reshape(16, 16, 128)
    csnd[:, 1] = times[:, 128:256].reshape(16, 16, 128)
    crcv[me] = csnd[me]
    lane = lax.broadcasted_iota(I32, (1, 64), 1)
    pos_row = jnp.full((1, 64), -1000, I32)
    for k in range(16):
        pos_row = jnp.where(lane == a * 16 + k, pos_ref[0, k], pos_row)
    pos_hot = (lax.broadcasted_iota(I32, (256, 64), 0) == pos_row + core * 128).astype(F32)
    own_lane = lax.broadcasted_iota(I32, (16, 64), 1) == a * 16 + lax.broadcasted_iota(I32, (16, 64), 0)

    def counts_ready():
        arrive(crcv.at[0:15], c_r, c_s)
        for i in range(4):
            for k in range(2):
                ct[i, k * 128 : (k + 1) * 128, :] = (
                    crcv[i * 4 : i * 4 + 4, k].astype(F32).reshape(64, 128).T
                )
        ct[b] = ct[b] + pos_hot

    def scores(*blocks):
        def rows_of(h):
            got = [qown[pl.ds(b_ * 4, 4), h].reshape(64, H) for b_ in blocks]
            return got[0] if len(got) == 1 else jnp.concatenate(got, axis=0)

        s = dot(pb[:, 0:H], rows_of(0), NT)
        s = (s + dot(pb[:, H:D], rows_of(1), NT)) * HEAT
        return [s[:, i * 64 : (i + 1) * 64] for i in range(len(blocks))]

    def statistics(b_, s):
        c = ct[b_]
        named = c > 0.0
        top = jnp.max(jnp.where(named, s, -1e30), axis=0, keepdims=True)
        e = c * jnp.exp(jnp.where(named, s - top, -1e30))
        est[b_] = e
        side = (lax.broadcasted_iota(I32, (1, 128), 1) >> 6) == lax.rem(b_, 2)
        sums = (top, jnp.sum(e, axis=0, keepdims=True), jnp.sum(e * s, axis=0, keepdims=True))
        for k, v in enumerate(sums):
            row = stat[b_ // 2, k : k + 1, :]
            stat[b_ // 2, k : k + 1, :] = jnp.where(side, jnp.concatenate([v, v], axis=1), row)

    pl.semaphore_wait(near_s.at[0], 2)
    tell_z(near_s.at[1], 2)
    pl.semaphore_wait(near_s.at[3], 4)
    tell_plane(near_s.at[4])
    got_half(slot(am, b), 0)
    q_half(slot(am, b), 0, at(ap, b))
    q_half(slot(am, b), 0, at(a, bp))
    got_half(slot(ap, b), 1)
    q_half(slot(ap, b), 1, at(am, b))
    q_half(slot(ap, b), 1, at(a, bm))
    pl.semaphore_wait(near_s.at[4], 4)
    tell_plane(near_s.at[5])
    got_half(slot(am, b), 1)
    q_half(slot(am, b), 1, at(a, bm))
    q_half(slot(am, b), 1, at(a, bp))
    got_half(slot(ap, b), 0)
    q_half(slot(ap, b), 0, at(a, bp))
    q_half(slot(ap, b), 0, at(a, bm))
    q_half(slot(am, b), 0, at(a, bm))
    q_half(slot(ap, b), 1, at(a, bp))
    q_other(slot(am, b))
    q_other(slot(ap, b))
    pl.semaphore_wait(near_s.at[1], 2)
    tell_z(near_s.at[2], 4)
    pl.semaphore_wait(near_s.at[5], 4)
    peers(lambda a_, b_, s: push(csnd.at[s], crcv.at[me], c_s, c_r, at(a_, b_)))
    got_half(slot(a2, b), 0)
    q_half(slot(a2, b), 0, at(a, bp))
    got_half(slot(a2, b), 1)
    q_half(slot(a2, b), 1, at(a, bm))
    q_half(slot(a2, b), 1, at(a, bp))
    q_half(slot(a2, b), 0, at(a, bm))
    q_other(slot(a2, b))
    got_half(slot(a, bm), 0)
    q_half(slot(a, bm), 0, at(a, bp))
    got_half(slot(a, bp), 1)
    q_half(slot(a, bp), 1, at(a, bm))
    pl.semaphore_wait(near_s.at[2], 2)

    @pl.loop(0, 15)
    def _(k):
        zk = lax.rem(z + lax.rem(k + 5, 15) + 1, 16)
        push(ab.at[kind, zcols], ab.at[kind, zcols], ab_s, ab_r, (dp, zk))

    arrive(pb.at[other_rows], p_r, p_s)
    (s_b,) = scores(b)
    for a_ in (am, ap):
        got_half(slot(a_, bm), 0)
        q_half(slot(a_, bm), 0, at(a, bp))
        got_half(slot(a_, bp), 1)
        q_half(slot(a_, bp), 1, at(a, bm))
    got_half(slot(a2, bm), 0)
    q_half(slot(a2, bm), 0, at(a, bp))
    got_half(slot(a2, bp), 1)
    q_half(slot(a2, bp), 1, at(a, bm))
    for a_ in (a, am, ap, a2):
        got_half(slot(a_, bm), 1)
        got_half(slot(a_, bp), 0)
        q_other(slot(a_, bm))
        q_other(slot(a_, bp))
    s_m, s_p = scores(bm, bp)
    counts_ready()
    s_pos = jnp.sum(pos_hot * s_b, axis=0, keepdims=True)
    statistics(b, s_b)
    statistics(bm, s_m)
    statistics(bp, s_p)
    for a_ in (a, am, ap, a2):
        for h in range(2):
            got_half(slot(a_, b2), h)
    (s_2,) = scores(b2)
    statistics(b2, s_2)
    peers(lambda a_, b_, s: push(stat, srcv.at[me], s_s, s_r, at(a_, b_)))
    srcv[me] = stat[...]
    for a_ in (a, am, ap, a2):
        q_other(slot(a_, b2))

    arrive(ab.at[kind, 0 : 15 * 256], ab_r, ab_s)
    ab_copy = push(ab.at[kind, :], ab.at[kind, :], abp_s, abp_r, partner)
    arrive(ab.at[other_kind, :], abp_r, abp_s)
    loads[6].wait()
    loads[7].wait()
    low_rows = dot(aq_ref[...], ab[0:16, :], NT).astype(BF16).astype(F32) * q_inv
    g_hi, g_lo = hi_lo(low_rows)
    gsnd[...] = jnp.zeros((16, 128), BF16)
    gsnd[:, 0:16] = g_hi
    gsnd[:, 16:32] = g_lo
    grcv[me] = gsnd[...]
    peers(lambda a_, b_, s: push(gsnd, grcv.at[me], g_s, g_r, at(a_, b_)))
    low_p = dot(ab[0:16, :], ap_ref[...], NT).astype(BF16)
    low_q = dot(ab[0:16, :], aq_ref[...], NT).astype(BF16)
    pbt = jnp.concatenate(hi_lo(dot(ab[16:32, :], pb[...], NT)), axis=0)
    block = pl.ds(b * 4, 4)
    ubt = dot(ab[16:32, 0:H], qown[block, 0].reshape(64, H), NT)
    ubt = ubt + dot(ab[16:32, H:D], qown[block, 1].reshape(64, H), NT)
    inv_row = jnp.sum(jnp.where(own_lane, q_inv, 0.0), axis=0, keepdims=True)

    arrive(srcv.at[0:15], s_r, s_s)

    top = srcv[0, :, 0:1, :]
    for s in range(1, 16):
        top = jnp.maximum(top, srcv[s, :, 0:1, :])
    total = jnp.zeros((2, 1, 128), F32)
    first = jnp.zeros((2, 1, 128), F32)
    for s in range(16):
        f = jnp.exp(srcv[s, :, 0:1, :] - top)
        total = total + f * srcv[s, :, 1:2, :]
        first = first + f * srcv[s, :, 2:3, :]
    rows_s[:, 0:1, :] = jnp.exp(stat[:, 0:1, :] - top) * (HEAT / total)
    rows_s[:, 1:2, :] = first / total
    for i in range(4):
        est[i] = est[i] * rows_s[i // 2, 0:1, i % 2 * 64 : i % 2 * 64 + 64]
    est[b] = est[b] - HEAT * pos_hot
    weight = jnp.concatenate([est[i] for i in range(4)], axis=1)
    w_hi, w_lo = hi_lo(weight)
    wt[0] = w_hi
    wt[1] = w_lo
    w_copy = push(wt.at[:, other_rows], woth, w_s, w_r, partner)
    mean = rows_s[b // 2, 1:2, :]
    inner_row = jnp.where(lax.rem(b, 2) == 0, mean[:, 0:64], mean[:, 64:128]) - s_pos
    inner = lanes_sum(jnp.where(own_lane, inner_row, 0.0))

    share = dot(pbt, w_hi) + dot(pbt, w_lo)
    share = share[0:16] + share[16:32]
    for i in range(4):
        ysnd[i, :, 0:64] = share[:, i * 64 : (i + 1) * 64]
    peers(lambda a_, b_, s: push(ysnd.at[b_], yrcv.at[me], y_s, y_r, at(a_, b_)))
    yrcv[me] = ysnd[b]
    wq_hi, wq_lo = hi_lo(weight.T)
    wq[0] = wq_hi
    wq[1] = wq_lo

    def shares(b_, h, put):
        rows = pl.ds(pl.multiple_of(b_ * 64, 64), 64)
        w = jnp.concatenate([wq[0, rows, :], wq[1, rows, :]], axis=0)
        for j in range(H // T):
            r = dot(w, pb[:, h * H + j * T : h * H + (j + 1) * T])
            put(slice(j * T, (j + 1) * T), (r[0:64] + r[64:128]).reshape(4, 16, T))

    def put_in(ref, *where):
        def put(cols, r):
            ref[(*where, slice(None), slice(None), cols)] = r.astype(ref.dtype)

        return put

    rs = []

    def hop(n, src, dst, device):
        rs.append(push(src, dst, rs_s.at[n], rs_r.at[n], device))

    def landed(dst, n):
        arrive(dst, rs_r.at[n], rs_s.at[0])

    shares(b2, 0, put_in(t1, 0))
    hop(0, t1.at[0], rl1.at[0], at(a, bp))
    shares(b2, 1, put_in(t1, 1))
    hop(1, t1.at[1], rl1.at[1], at(a, bm))
    shares(bp, 1, put_in(d1p, 1))
    hop(2, d1p.at[1], r1m.at[1], at(a, bp))
    shares(bm, 0, put_in(d1m, 0))
    hop(3, d1m.at[0], r1p.at[0], at(a, bm))

    arrive(grcv.at[0:15], g_r, g_s)
    gall = grcv[...].reshape(256, 128)
    xt = (dot(wt[0], gall) + dot(wt[1], gall)).T
    xs = jnp.concatenate(hi_lo(xt[0:16] + xt[16:32]), axis=0)

    def two_parts(w, q, h, sub):
        r = dot(w, q[:, h, :, sub].reshape(256, T))
        return r[0:128] + r[128:256]

    wa = jnp.concatenate([wt[0, own_rows, :], wt[1, own_rows, :]], axis=0)
    for h in range(2):
        for j in range(H // T):
            cols = slice(h * H + j * T, h * H + (j + 1) * T)
            pup[:, cols] = two_parts(wa, qown, h, slice(j * T, (j + 1) * T))
            r = dot(xs, pb[:, cols])
            dsum[16:32, cols] = r[0:16] + r[16:32]
    arrive(qoth, qo_r, ag_s.at[1])
    arrive(woth, w_r, w_s)
    wb = jnp.concatenate([woth[0], woth[1]], axis=0)
    p_in = jnp.zeros((128, 1), F32)
    for h in range(2):
        for j in range(H // T):
            cols = slice(h * H + j * T, h * H + (j + 1) * T)
            r = pup[:, cols] + two_parts(wb, qoth, h, slice(j * T, (j + 1) * T))
            p_in = p_in + lanes_sum(p_ref[:, cols].astype(F32) * r)
            pup[:, cols] = r
    p_inv = pinv[:, 0:1]
    p_in = p_in * p_inv * p_inv
    for j in range(D // T):
        cols = slice(j * T, (j + 1) * T)
        gp_ref[:, cols] = ((pup[:, cols] - p_ref[:, cols].astype(F32) * p_in) * p_inv).astype(BF16)
    gp_out = pltpu.make_async_copy(gp_ref, gp_hbm, out_s.at[0])
    gp_out.start()

    back_p = dot(ab[16:32, :], gp_ref[...], NT).astype(BF16)
    arrive(yrcv.at[0:15], y_r, y_s)
    ysum = yrcv[0, :, 0:64]
    for s in range(1, 16):
        ysum = ysum + yrcv[s, :, 0:64]
    back = ((ysum - inner_row * ubt) * inv_row).astype(BF16)
    pick = lax.broadcasted_iota(I32, (64, 16), 0) == a * 16 + lax.broadcasted_iota(I32, (64, 16), 1)
    back_q = dot(back, pick.astype(F32).astype(BF16)).astype(BF16)
    back_all = jnp.concatenate([back_p, back_q], axis=1)
    low_all = jnp.concatenate([low_p, -low_q], axis=1)
    for j in range(D // T):
        cols = slice(j * T, (j + 1) * T)
        r = dot(back_all, jnp.concatenate([ap_ref[:, cols], aq_ref[:, cols]], axis=0))
        dsum[0:16, cols] = ADAPTER_SCALE * r
        v2 = (q_ref[:, cols].astype(F32) * (inner * q_inv * q_inv)).astype(BF16)
        r = dot(low_all, jnp.concatenate([gp_ref[:, cols], v2], axis=0))
        dsum[16:32, cols] = ADAPTER_SCALE * (dsum[16:32, cols] + r)
    mine = pl.ds(pl.multiple_of(core * 16, 16), 16)
    theirs = pl.ds(pl.multiple_of(other * 16, 16), 16)
    d_copy = push(dsum.at[theirs], dbuf, d_s, d_r, partner)

    shares(bp, 0, put_in(uf, 0))
    shares(bm, 1, put_in(uf, 1))

    arrive(dbuf, d_r, d_s)
    for j in range(D // 128):
        cols = slice(j * 128, (j + 1) * 128)
        drow[:, j // 2, j % 2, :] = dsum[mine, cols] + dbuf[:, cols]
    peers(lambda a_, b_, s: push(drow.at[s], rrow.at[me], rr_s, rr_r, at(a_, b_)))
    rrow[me] = drow[me]
    landed(rl1.at[0], 0)
    d1p[0] = (uf[0] + rl1[0].astype(F32)).astype(BF16)
    hop(4, d1p.at[0], r1m.at[0], at(a, bp))
    landed(rl1.at[1], 1)
    d1m[1] = (uf[1] + rl1[1].astype(F32)).astype(BF16)
    hop(5, d1m.at[1], r1p.at[1], at(a, bm))
    shares(b, 0, put_in(v1, 0))
    shares(b, 1, put_in(v1, 1))
    arrive(rrow.at[0:15], rr_r, rr_s)
    acc = rrow[0]
    for s in range(1, 16):
        acc = acc + rrow[s]
    zrow[...] = acc

    @pl.loop(0, 15)
    def _(k):
        zk = lax.rem(z + lax.rem(k + 4, 15) + 1, 16)
        push(zrow.at[zk], zbuf.at[z], z_s, z_r, (dp, zk))

    zbuf[z] = zrow[z]

    landed(r1m.at[1], 2)
    landed(r1p.at[0], 3)
    landed(r1m.at[0], 4)
    landed(r1p.at[1], 5)
    for h in range(2):
        v1[h] = v1[h] + r1m[h].astype(F32) + r1p[h].astype(F32)
        t2[h] = v1[h, a2].astype(BF16)
        if h == 0:
            hop(6, t2.at[0], rl2.at[0], at(ap, b))
            d2m[0] = v1[0, am].astype(BF16)
            hop(7, d2m.at[0], r2p.at[0], at(am, b))
        else:
            hop(8, t2.at[1], rl2.at[1], at(am, b))
            d2p[1] = v1[1, ap].astype(BF16)
            hop(9, d2p.at[1], r2m.at[1], at(ap, b))
    landed(rl2.at[0], 6)
    d2p[0] = (v1[0, ap] + rl2[0].astype(F32)).astype(BF16)
    hop(10, d2p.at[0], r2m.at[0], at(ap, b))
    landed(rl2.at[1], 8)
    d2m[1] = (v1[1, am] + rl2[1].astype(F32)).astype(BF16)
    hop(11, d2m.at[1], r2p.at[1], at(am, b))
    arrive(zbuf.at[0:15], z_r, z_s)
    acc = zbuf[0]
    for s in range(1, 16):
        acc = acc + zbuf[s]
    orow[...] = acc
    oall[core * 16 + me] = acc

    def back_to_all(a_, b_, s):
        row = core * 16 + me
        push(orow, oall.at[row], o_s, o_r, at(a_, b_))
        push(orow, oall.at[row], o_s, o_r, (a_ * sa + b_ * sb + other, z))

    peers(back_to_all)
    push(orow, oall.at[core * 16 + me], o_s, o_r, partner)

    landed(r2p.at[0], 7)
    landed(r2m.at[1], 9)
    landed(r2m.at[0], 10)
    landed(r2p.at[1], 11)
    qu = jnp.concatenate(
        [v1[h, a] + r2m[h].astype(F32) + r2p[h].astype(F32) for h in range(2)], axis=1
    )
    qv = q_ref[...].astype(F32)
    q_inv = 1.0 / jnp.sqrt(lanes_sum(qv * qv) + EPSILON)
    q_in = lanes_sum(qv * qu) * q_inv * q_inv
    gq_ref[...] = ((qu - qv * q_in) * q_inv).astype(BF16)
    gq_out = pltpu.make_async_copy(gq_ref, gq_hbm, out_s.at[1])
    gq_out.start()

    for c in rs + [p_copy, d_copy, w_copy, ab_copy]:
        c.wait_send()
    gone(qown.at[0:15], ag_s.at[0], q_r.at[0, 0])
    gone(qown, ag_s.at[1], qo_r)
    gone(ab.at[kind, 0 : 15 * 256], ab_s, ab_r)
    gone(csnd.at[0:15], c_s, c_r)
    gone(srcv.at[0:15], s_s, s_r)
    gone(grcv.at[0:15], g_s, g_r)
    gone(yrcv.at[0:15], y_s, y_r)
    gone(drow.at[0:15], rr_s, rr_r)
    gone(zrow.at[0:15], z_s, z_r)
    gone(oall.at[0:31], o_s, o_r)
    arrive(oall.at[0:31], o_r, o_s)
    outs = [gp_out, gq_out]
    for c_, dst in ((0, down_hbm), (1, up_hbm)):
        dv[c_, :, 0:128] = oall[c_ * 16 : c_ * 16 + 16, 0, :]
        dv[c_, :, 128:256] = oall[c_ * 16 : c_ * 16 + 16, 1, :]
        outs.append(pltpu.make_async_copy(dv.at[c_], dst, out_s.at[2 + c_]))
        outs[-1].start()

    for c in outs:
        c.wait()


def hand_over(*refs):
    copies = [pltpu.make_async_copy(refs[i], refs[4 + i], refs[8].at[i]) for i in (1, 0, 2, 3)]
    for c in copies:
        c.start()
    for c in copies:
        c.wait()


ANY = pl.BlockSpec(memory_space=pl.ANY)


def per_device(query, passage, query_attn, passage_attn, positives, negatives, home, down, up):
    dma = pltpu.SemaphoreType.DMA
    vm = pltpu.VMEM
    half = vm((2, 4, 16, H), BF16)
    row = vm((2, 16, H), BF16)
    grad_q, grad_p, sum_down, sum_up = pl.pallas_call(
        kernel,
        out_shape=(
            jax.ShapeDtypeStruct((16, D), BF16),
            jax.ShapeDtypeStruct((128, D), BF16),
            jax.ShapeDtypeStruct((16, 256), F32),
            jax.ShapeDtypeStruct((16, 256), F32),
        ),
        in_specs=[pl.BlockSpec(memory_space=pltpu.HBM)] * 9,
        out_specs=(ANY,) * 4,
        scratch_shapes=[
            vm((16, D), BF16),
            vm((128, D), BF16),
            vm((16, D), BF16),
            vm((128, D), BF16),
            vm((16, 64), I32),
            vm((32, 128), I32),
            vm((16, 256), BF16),
            vm((16, 256), BF16),
            pltpu.SMEM((1, 16), I32),
            vm((16, D), BF16),
            vm((128, D), BF16),
            vm((2, 16, 256), F32),
            vm((16, 2, 16, H), BF16),
            vm((16, 2, 16, H), BF16),
            vm((256, D), BF16),
            vm((32, D), BF16),
            vm((16, 128), I32),
            vm((256, H), BF16),
            vm((256, H), BF16),
            vm((16, 2, 16, 128), BF16),
            vm((16, 2, 16, 128), BF16),
            vm((4, 256, 64), F32),
            vm((4, 256, 64), F32),
            vm((2, 4, 128), F32),
            vm((16, 2, 4, 128), F32),
            vm((2, 4, 128), F32),
            vm((2, 256, 256), BF16),
            vm((2, 128, 256), BF16),
            vm((2, 256, 256), BF16),
            vm((16, 128), BF16),
            vm((16, 16, 128), BF16),
            vm((4, 16, 128), F32),
            vm((16, 16, 128), F32),
            half,
            half,
            half,
            half,
            half,
            half,
            vm((2, 4, 16, H), F32),
            vm((2, 4, 16, H), F32),
            row,
            row,
            row,
            row,
            row,
            row,
            vm((128, 128), F32),
            vm((128, D), F32),
            vm((32, D), F32),
            vm((16, D), F32),
            vm((16, 16, 2, 128), F32),
            vm((16, 16, 2, 128), F32),
            vm((16, 2, 128), F32),
            vm((16, 2, 128), F32),
            vm((2, 128), F32),
            vm((32, 2, 128), F32),
            dma((9,)),
            dma((4,)),
            dma((2,)),
            dma((16, 2)),
            dma(()),
            dma(()),
            dma(()),
            dma(()),
            dma(()),
            dma(()),
            dma(()),
            pltpu.SemaphoreType.REGULAR((6,)),
            dma(()),
            dma(()),
            dma(()),
            dma(()),
            dma(()),
            dma(()),
            dma(()),
            dma(()),
            dma(()),
            dma(()),
            dma((12,)),
            dma((12,)),
            dma(()),
            dma(()),
            dma(()),
            dma(()),
            dma(()),
            dma(()),
            dma(()),
            dma(()),
        ],
        compiler_params=pltpu.CompilerParams(
            collective_id=0, has_side_effects=True, vmem_limit_bytes=26 * 1024 * 1024
        ),
    )(
        *(
            pltpu.with_memory_space_constraint(v, pltpu.HBM)
            for v in (
                query[0], passage[0], query_attn[0], passage_attn[0], negatives[0],
                home[0].reshape(32, 128), down, up, positives,
            )
        )
    )
    outs = pl.pallas_call(
        hand_over,
        out_shape=tuple(jax.ShapeDtypeStruct(v.shape, v.dtype) for v in (grad_q, grad_p, sum_down, sum_up)),
        in_specs=[ANY] * 4,
        out_specs=(ANY,) * 4,
        scratch_shapes=[dma((4,))],
        compiler_params=pltpu.CompilerParams(vmem_limit_bytes=1024 * 1024),
    )(grad_q, grad_p, sum_down, sum_up)
    return outs[0][None], outs[1][None], outs[2], outs[3]


def solution(mesh):
    in_specs = (
        P("fsdp", "dp", None),
        P("fsdp", "dp", None),
        P("fsdp", "dp", None),
        P("fsdp", "dp", None),
        P("fsdp", "dp"),
        P("fsdp", "dp", None),
        P("fsdp", None),
        P(None, "fsdp"),
        P(None, "fsdp"),
    )
    out_specs = (P("fsdp", "dp", None), P("fsdp", "dp", None), P(None, "fsdp"), P(None, "fsdp"))
    return jax.shard_map(
        per_device, mesh=mesh, in_specs=in_specs, out_specs=out_specs, check_vma=False
    )
```

```python
import jax
import jax.numpy as jnp
from jax import lax
from jax.experimental import pallas as pl
from jax.experimental.pallas import tpu as pltpu
from jax.sharding import PartitionSpec as P

MESH = pl.DeviceIdType.MESH
F32, BF16, I32 = jnp.float32, jnp.bfloat16, jnp.int32
HEAT = 100.0
ADAPTER_SCALE = 2.0
EPSILON = 1e-06
D = 4096
H = 2048
T = 512
NN = (((1,), (0,)), ((), ()))
NT = (((1,), (1,)), ((), ()))


def dot(lhs, rhs, dims=NN):
    return lax.dot_general(lhs, rhs, dims, preferred_element_type=F32)


def hi_lo(w):
    hi = w.astype(BF16)
    return hi, (w - hi.astype(F32)).astype(BF16)


def lanes_sum(v):
    return jnp.sum(v, axis=-1, keepdims=True)


def kernel(
    q_hbm, p_hbm, aq_hbm, ap_hbm, neg_hbm, home_hbm, aw_hbm, bw_hbm, pos_hbm,
    gq_hbm, gp_hbm, down_hbm, up_hbm,
    q_ref, p_ref, aq_ref, ap_ref, neg_ref, home_ref, aw_ref, bw_ref, pos_ref, gq_ref, gp_ref, dv,
    qown, qoth, pb, ab, negp, lhs, rhs, csnd, crcv, ct, est, stat, srcv, rows_s,
    wt, woth, wq, gsnd, grcv, ysnd, yrcv,
    t1, rl1, d1p, d1m, r1m, r1p, uf, v1, t2, rl2, d2p, d2m, r2m, r2p,
    pinv, pup, dsum, dbuf, drow, rrow, zrow, zbuf, orow, oall,
    in_s, out_s, ag_s, q_r, qo_r, p_s, p_r, ab_s, ab_r, abp_s, abp_r, near_s, c_s, c_r, s_s, s_r, w_s, w_r, g_s, g_r, y_s, y_r,
    rs_s, rs_r, d_s, d_r, rr_s, rr_r, z_s, z_r, o_s, o_r,
):
    dp, z = lax.axis_index("dp"), lax.axis_index("fsdp")
    core, chip = lax.rem(dp, 2), dp // 2
    x, y = chip // 4, lax.rem(chip, 4)
    a = x * (1 - core) + y * core
    b = y * (1 - core) + x * core
    sa, sb = 8 - 6 * core, 2 + 6 * core
    other = 1 - core

    def near(v, k):
        return lax.rem(v + k, 4)

    def at(a_, b_):
        return (a_ * sa + b_ * sb + core, z)

    def slot(a_, b_):
        return b_ * 4 + a_

    me = slot(a, b)
    partner = (chip * 2 + other, z)
    am, a2, ap = near(a, 3), near(a, 2), near(a, 1)
    bm, b2, bp = near(b, 3), near(b, 2), near(b, 1)

    barrier = pltpu.get_barrier_semaphore()

    loads = [
        pltpu.make_async_copy(src, dst, in_s.at[i])
        for i, (src, dst) in enumerate(
            (
                (q_hbm, q_ref), (p_hbm, p_ref), (aw_hbm, aw_ref), (bw_hbm, bw_ref),
                (neg_hbm, neg_ref), (home_hbm, home_ref), (aq_hbm, aq_ref), (ap_hbm, ap_ref), (pos_hbm, pos_ref),
            )
        )
    ]
    loads[0].start()
    loads[1].start()

    def tell_plane(sem):
        for device in (at(ap, b), at(am, b), at(a, bp), at(a, bm)):
            pl.semaphore_signal(sem, inc=1, device_id=device, device_id_type=MESH)

    pl.semaphore_signal(barrier, inc=1, device_id=partner, device_id_type=MESH)
    tell_plane(barrier)

    def tell_z(sem, step):
        for k in (step, 16 - step):
            pl.semaphore_signal(sem, inc=1, device_id=(dp, lax.rem(z + k, 16)), device_id_type=MESH)

    tell_z(barrier, 1)

    for c in loads[2:]:
        c.start()

    loads[0].wait()
    qv = q_ref[...].astype(F32)
    q_inv = 1.0 / jnp.sqrt(lanes_sum(qv * qv) + EPSILON)
    qe = (qv * q_inv).astype(BF16)
    qown[me, 0] = qe[:, :H]
    qown[me, 1] = qe[:, H:]
    pl.semaphore_wait(barrier, 7)
    tell_z(near_s.at[0], 1)
    tell_plane(near_s.at[3])

    def push(src, dst, ssem, rsem, device):
        c = pltpu.make_async_remote_copy(
            src_ref=src, dst_ref=dst, send_sem=ssem, recv_sem=rsem, device_id=device, device_id_type=MESH
        )
        c.start()
        return c

    def arrive(dst, rsem, ssem):
        pltpu.make_async_remote_copy(
            src_ref=dst, dst_ref=dst, send_sem=ssem, recv_sem=rsem, device_id=partner, device_id_type=MESH
        ).wait_recv()

    def gone(src, ssem, rsem):
        pltpu.make_async_remote_copy(
            src_ref=src, dst_ref=src, send_sem=ssem, recv_sem=rsem, device_id=partner, device_id_type=MESH
        ).wait_send()

    def peers(body):
        def one(k):
            a_, b_ = near(a, lax.rem(6 - lax.rem(k, 4), 4)), near(b, lax.rem(6 - k // 4, 4))
            body(a_, b_, slot(a_, b_))

        pl.loop(0, 10)(one)
        pl.loop(11, 16)(one)

    def q_half(s, h, device):
        push(qown.at[s, h], qown.at[s, h], ag_s.at[0], q_r.at[s, h], device)

    def q_other(s):
        push(qown.at[s], qoth.at[s], ag_s.at[1], qo_r, partner)

    def got_half(s, h):
        arrive(qown.at[s, h], q_r.at[s, h], ag_s.at[0])

    q_half(me, 0, at(ap, b))
    q_half(me, 1, at(am, b))
    q_half(me, 1, at(ap, b))
    q_half(me, 0, at(am, b))
    for i in (2, 3):
        loads[i].wait()
    zcols = pl.ds(pl.multiple_of(z * 256, 256), 256)
    kind = pl.ds(pl.multiple_of(core * 16, 16), 16)
    other_kind = pl.ds(pl.multiple_of(other * 16, 16), 16)
    ab[kind, zcols] = jnp.where(core == 0, aw_ref[...], bw_ref[...])
    loads[1].wait()

    def p_rows(i, carry):
        rows = pl.ds(pl.multiple_of(i * 32, 32), 32)
        pv = p_ref[rows, :].astype(F32)
        inv = 1.0 / jnp.sqrt(lanes_sum(pv * pv) + EPSILON)
        pinv[rows, :] = jnp.broadcast_to(inv, (32, 128))
        dst = pl.ds(pl.multiple_of(core * 128 + i * 32, 32), 32)
        pb[dst, :] = (pv * inv).astype(BF16)
        return carry

    lax.fori_loop(0, 4, p_rows, 0)
    own_rows = pl.ds(pl.multiple_of(core * 128, 128), 128)
    other_rows = pl.ds(pl.multiple_of(other * 128, 128), 128)
    p_copy = push(pb.at[own_rows], pb.at[own_rows], p_s, p_r, partner)
    q_other(me)

    q_half(me, 0, at(a, bp))
    q_half(me, 1, at(a, bm))
    q_half(me, 1, at(a, bp))
    q_half(me, 0, at(a, bm))

    loads[4].wait()
    loads[5].wait()
    loads[8].wait()
    negp[...] = jnp.full((16, 128), -1, I32)
    negp[:, 0:64] = neg_ref[...]
    n_row = jnp.concatenate([negp[k : k + 1, :] for k in range(16)], axis=1)
    home = home_ref[...]
    table = jnp.concatenate(
        [(home >> 7).astype(F32).T, (home & 127).astype(F32).T], axis=0
    ).astype(BF16)
    for part in range(4):
        n = n_row[:, part * T : (part + 1) * T]
        lane_q = (lax.broadcasted_iota(I32, (1, T), 1) >> 7) + part * 4
        picked = (lax.broadcasted_iota(I32, (32, T), 0) == (n >> 7)).astype(F32).astype(BF16)
        found = dot(table, picked)
        low = lax.broadcasted_iota(I32, (128, T), 0) == (n & 127)
        dev_row = jnp.sum(jnp.where(low, found[0:128], 0.0), axis=0, keepdims=True).astype(I32)
        in_dev = jnp.sum(jnp.where(low, found[128:256], 0.0), axis=0, keepdims=True).astype(I32)
        chip_row = dev_row >> 1
        key = ((chip_row >> 2) * (1 + 3 * core) + (chip_row & 3) * (4 - 3 * core)) * 16 + lane_q
        key = jnp.where(n >= 0, key, -1)
        col = (dev_row & 1) * 128 + in_dev
        rows = lax.broadcasted_iota(I32, (256, T), 0)
        lhs[:, part * T : (part + 1) * T] = (rows == key).astype(F32).astype(BF16)
        rhs[:, part * T : (part + 1) * T] = (rows == col).astype(F32).astype(BF16)
    times = dot(lhs[...], rhs[...], NT).astype(BF16)
    csnd[:, 0] = times[:, 0:128].reshape(16, 16, 128)
    csnd[:, 1] = times[:, 128:256].reshape(16, 16, 128)
    crcv[me] = csnd[me]
    lane = lax.broadcasted_iota(I32, (1, 64), 1)
    pos_row = jnp.full((1, 64), -1000, I32)
    for k in range(16):
        pos_row = jnp.where(lane == a * 16 + k, pos_ref[0, k], pos_row)
    pos_hot = (lax.broadcasted_iota(I32, (256, 64), 0) == pos_row + core * 128).astype(F32)
    own_lane = lax.broadcasted_iota(I32, (16, 64), 1) == a * 16 + lax.broadcasted_iota(I32, (16, 64), 0)

    def counts_ready():
        arrive(crcv.at[0:15], c_r, c_s)
        for i in range(4):
            for k in range(2):
                ct[i, k * 128 : (k + 1) * 128, :] = (
                    crcv[i * 4 : i * 4 + 4, k].astype(F32).reshape(64, 128).T
                )
        ct[b] = ct[b] + pos_hot

    def scores(*blocks):
        def rows_of(h):
            got = [qown[pl.ds(b_ * 4, 4), h].reshape(64, H) for b_ in blocks]
            return got[0] if len(got) == 1 else jnp.concatenate(got, axis=0)

        s = dot(pb[:, 0:H], rows_of(0), NT)
        s = (s + dot(pb[:, H:D], rows_of(1), NT)) * HEAT
        return [s[:, i * 64 : (i + 1) * 64] for i in range(len(blocks))]

    def statistics(b_, s):
        c = ct[b_]
        named = c > 0.0
        top = jnp.max(jnp.where(named, s, -1e30), axis=0, keepdims=True)
        e = c * jnp.exp(jnp.where(named, s - top, -1e30))
        est[b_] = e
        side = (lax.broadcasted_iota(I32, (1, 128), 1) >> 6) == lax.rem(b_, 2)
        sums = (top, jnp.sum(e, axis=0, keepdims=True), jnp.sum(e * s, axis=0, keepdims=True))
        for k, v in enumerate(sums):
            row = stat[b_ // 2, k : k + 1, :]
            stat[b_ // 2, k : k + 1, :] = jnp.where(side, jnp.concatenate([v, v], axis=1), row)

    pl.semaphore_wait(near_s.at[0], 2)
    tell_z(near_s.at[1], 2)
    pl.semaphore_wait(near_s.at[3], 4)
    tell_plane(near_s.at[4])
    got_half(slot(am, b), 0)
    q_half(slot(am, b), 0, at(ap, b))
    q_half(slot(am, b), 0, at(a, bp))
    got_half(slot(ap, b), 1)
    q_half(slot(ap, b), 1, at(am, b))
    q_half(slot(ap, b), 1, at(a, bm))
    pl.semaphore_wait(near_s.at[4], 4)
    tell_plane(near_s.at[5])
    got_half(slot(am, b), 1)
    q_half(slot(am, b), 1, at(a, bm))
    q_half(slot(am, b), 1, at(a, bp))
    got_half(slot(ap, b), 0)
    q_half(slot(ap, b), 0, at(a, bp))
    q_half(slot(ap, b), 0, at(a, bm))
    q_half(slot(am, b), 0, at(a, bm))
    q_half(slot(ap, b), 1, at(a, bp))
    q_other(slot(am, b))
    q_other(slot(ap, b))
    pl.semaphore_wait(near_s.at[1], 2)
    tell_z(near_s.at[2], 4)
    pl.semaphore_wait(near_s.at[5], 4)
    peers(lambda a_, b_, s: push(csnd.at[s], crcv.at[me], c_s, c_r, at(a_, b_)))
    got_half(slot(a2, b), 0)
    q_half(slot(a2, b), 0, at(a, bp))
    got_half(slot(a2, b), 1)
    q_half(slot(a2, b), 1, at(a, bm))
    q_half(slot(a2, b), 1, at(a, bp))
    q_half(slot(a2, b), 0, at(a, bm))
    q_other(slot(a2, b))
    got_half(slot(a, bm), 0)
    q_half(slot(a, bm), 0, at(a, bp))
    got_half(slot(a, bp), 1)
    q_half(slot(a, bp), 1, at(a, bm))
    pl.semaphore_wait(near_s.at[2], 2)

    @pl.loop(0, 15)
    def _(k):
        zk = lax.rem(z + lax.rem(k + 5, 15) + 1, 16)
        push(ab.at[kind, zcols], ab.at[kind, zcols], ab_s, ab_r, (dp, zk))

    for a_ in (am, ap):
        got_half(slot(a_, bm), 0)
        q_half(slot(a_, bm), 0, at(a, bp))
        got_half(slot(a_, bp), 1)
        q_half(slot(a_, bp), 1, at(a, bm))
    arrive(pb.at[other_rows], p_r, p_s)
    (s_b,) = scores(b)
    got_half(slot(a2, bm), 0)
    q_half(slot(a2, bm), 0, at(a, bp))
    got_half(slot(a2, bp), 1)
    q_half(slot(a2, bp), 1, at(a, bm))
    for a_ in (a, am, ap, a2):
        got_half(slot(a_, bm), 1)
        got_half(slot(a_, bp), 0)
        q_other(slot(a_, bm))
        q_other(slot(a_, bp))
    s_m, s_p = scores(bm, bp)
    counts_ready()
    s_pos = jnp.sum(pos_hot * s_b, axis=0, keepdims=True)
    statistics(b, s_b)
    statistics(bm, s_m)
    statistics(bp, s_p)
    for a_ in (a, am, ap, a2):
        for h in range(2):
            got_half(slot(a_, b2), h)
    (s_2,) = scores(b2)
    statistics(b2, s_2)
    peers(lambda a_, b_, s: push(stat, srcv.at[me], s_s, s_r, at(a_, b_)))
    srcv[me] = stat[...]
    for a_ in (a, am, ap, a2):
        q_other(slot(a_, b2))

    arrive(ab.at[kind, 0 : 15 * 256], ab_r, ab_s)
    ab_copy = push(ab.at[kind, :], ab.at[kind, :], abp_s, abp_r, partner)
    arrive(ab.at[other_kind, :], abp_r, abp_s)
    loads[6].wait()
    loads[7].wait()
    low_rows = dot(aq_ref[...], ab[0:16, :], NT).astype(BF16).astype(F32) * q_inv
    g_hi, g_lo = hi_lo(low_rows)
    gsnd[...] = jnp.zeros((16, 128), BF16)
    gsnd[:, 0:16] = g_hi
    gsnd[:, 16:32] = g_lo
    grcv[me] = gsnd[...]
    peers(lambda a_, b_, s: push(gsnd, grcv.at[me], g_s, g_r, at(a_, b_)))
    low_p = dot(ab[0:16, :], ap_ref[...], NT).astype(BF16)
    low_q = dot(ab[0:16, :], aq_ref[...], NT).astype(BF16)
    pbt = jnp.concatenate(hi_lo(dot(ab[16:32, :], pb[...], NT)), axis=0)
    block = pl.ds(b * 4, 4)
    ubt = dot(ab[16:32, 0:H], qown[block, 0].reshape(64, H), NT)
    ubt = ubt + dot(ab[16:32, H:D], qown[block, 1].reshape(64, H), NT)
    inv_row = jnp.sum(jnp.where(own_lane, q_inv, 0.0), axis=0, keepdims=True)

    arrive(srcv.at[0:15], s_r, s_s)

    top = srcv[0, :, 0:1, :]
    for s in range(1, 16):
        top = jnp.maximum(top, srcv[s, :, 0:1, :])
    total = jnp.zeros((2, 1, 128), F32)
    first = jnp.zeros((2, 1, 128), F32)
    for s in range(16):
        f = jnp.exp(srcv[s, :, 0:1, :] - top)
        total = total + f * srcv[s, :, 1:2, :]
        first = first + f * srcv[s, :, 2:3, :]
    rows_s[:, 0:1, :] = jnp.exp(stat[:, 0:1, :] - top) * (HEAT / total)
    rows_s[:, 1:2, :] = first / total
    for i in range(4):
        est[i] = est[i] * rows_s[i // 2, 0:1, i % 2 * 64 : i % 2 * 64 + 64]
    est[b] = est[b] - HEAT * pos_hot
    weight = jnp.concatenate([est[i] for i in range(4)], axis=1)
    w_hi, w_lo = hi_lo(weight)
    wt[0] = w_hi
    wt[1] = w_lo
    w_copy = push(wt.at[:, other_rows], woth, w_s, w_r, partner)
    mean = rows_s[b // 2, 1:2, :]
    inner_row = jnp.where(lax.rem(b, 2) == 0, mean[:, 0:64], mean[:, 64:128]) - s_pos
    inner = lanes_sum(jnp.where(own_lane, inner_row, 0.0))

    share = dot(pbt, w_hi) + dot(pbt, w_lo)
    share = share[0:16] + share[16:32]
    for i in range(4):
        ysnd[i, :, 0:64] = share[:, i * 64 : (i + 1) * 64]
    peers(lambda a_, b_, s: push(ysnd.at[b_], yrcv.at[me], y_s, y_r, at(a_, b_)))
    yrcv[me] = ysnd[b]
    wq_hi, wq_lo = hi_lo(weight.T)
    wq[0] = wq_hi
    wq[1] = wq_lo

    def shares(b_, h, put):
        rows = pl.ds(pl.multiple_of(b_ * 64, 64), 64)
        w = jnp.concatenate([wq[0, rows, :], wq[1, rows, :]], axis=0)
        for j in range(H // T):
            r = dot(w, pb[:, h * H + j * T : h * H + (j + 1) * T])
            put(slice(j * T, (j + 1) * T), (r[0:64] + r[64:128]).reshape(4, 16, T))

    def put_in(ref, *where):
        def put(cols, r):
            ref[(*where, slice(None), slice(None), cols)] = r.astype(ref.dtype)

        return put

    rs = []

    def hop(n, src, dst, device):
        rs.append(push(src, dst, rs_s.at[n], rs_r.at[n], device))

    def landed(dst, n):
        arrive(dst, rs_r.at[n], rs_s.at[0])

    shares(b2, 0, put_in(t1, 0))
    hop(0, t1.at[0], rl1.at[0], at(a, bp))
    shares(b2, 1, put_in(t1, 1))
    hop(1, t1.at[1], rl1.at[1], at(a, bm))

    arrive(grcv.at[0:15], g_r, g_s)
    gall = grcv[...].reshape(256, 128)
    xt = (dot(wt[0], gall) + dot(wt[1], gall)).T
    xs = jnp.concatenate(hi_lo(xt[0:16] + xt[16:32]), axis=0)

    def two_parts(w, q, h, sub):
        r = dot(w, q[:, h, :, sub].reshape(256, T))
        return r[0:128] + r[128:256]

    wa = jnp.concatenate([wt[0, own_rows, :], wt[1, own_rows, :]], axis=0)
    for h in range(2):
        for j in range(H // T):
            cols = slice(h * H + j * T, h * H + (j + 1) * T)
            pup[:, cols] = two_parts(wa, qown, h, slice(j * T, (j + 1) * T))
            r = dot(xs, pb[:, cols])
            dsum[16:32, cols] = r[0:16] + r[16:32]
    arrive(qoth, qo_r, ag_s.at[1])
    arrive(woth, w_r, w_s)
    wb = jnp.concatenate([woth[0], woth[1]], axis=0)
    p_in = jnp.zeros((128, 1), F32)
    for h in range(2):
        for j in range(H // T):
            cols = slice(h * H + j * T, h * H + (j + 1) * T)
            r = pup[:, cols] + two_parts(wb, qoth, h, slice(j * T, (j + 1) * T))
            p_in = p_in + lanes_sum(p_ref[:, cols].astype(F32) * r)
            pup[:, cols] = r
    p_inv = pinv[:, 0:1]
    p_in = p_in * p_inv * p_inv
    for j in range(D // T):
        cols = slice(j * T, (j + 1) * T)
        gp_ref[:, cols] = ((pup[:, cols] - p_ref[:, cols].astype(F32) * p_in) * p_inv).astype(BF16)
    gp_out = pltpu.make_async_copy(gp_ref, gp_hbm, out_s.at[0])
    gp_out.start()

    back_p = dot(ab[16:32, :], gp_ref[...], NT).astype(BF16)
    arrive(yrcv.at[0:15], y_r, y_s)
    ysum = yrcv[0, :, 0:64]
    for s in range(1, 16):
        ysum = ysum + yrcv[s, :, 0:64]
    back = ((ysum - inner_row * ubt) * inv_row).astype(BF16)
    pick = lax.broadcasted_iota(I32, (64, 16), 0) == a * 16 + lax.broadcasted_iota(I32, (64, 16), 1)
    back_q = dot(back, pick.astype(F32).astype(BF16)).astype(BF16)
    back_all = jnp.concatenate([back_p, back_q], axis=1)
    low_all = jnp.concatenate([low_p, -low_q], axis=1)
    for j in range(D // T):
        cols = slice(j * T, (j + 1) * T)
        r = dot(back_all, jnp.concatenate([ap_ref[:, cols], aq_ref[:, cols]], axis=0))
        dsum[0:16, cols] = ADAPTER_SCALE * r
        v2 = (q_ref[:, cols].astype(F32) * (inner * q_inv * q_inv)).astype(BF16)
        r = dot(low_all, jnp.concatenate([gp_ref[:, cols], v2], axis=0))
        dsum[16:32, cols] = ADAPTER_SCALE * (dsum[16:32, cols] + r)
    mine = pl.ds(pl.multiple_of(core * 16, 16), 16)
    theirs = pl.ds(pl.multiple_of(other * 16, 16), 16)
    d_copy = push(dsum.at[theirs], dbuf, d_s, d_r, partner)

    shares(bp, 1, put_in(d1p, 1))
    shares(bm, 0, put_in(d1m, 0))
    shares(bp, 0, put_in(uf, 0))
    shares(bm, 1, put_in(uf, 1))

    arrive(dbuf, d_r, d_s)
    for j in range(D // 128):
        cols = slice(j * 128, (j + 1) * 128)
        drow[:, j // 2, j % 2, :] = dsum[mine, cols] + dbuf[:, cols]
    peers(lambda a_, b_, s: push(drow.at[s], rrow.at[me], rr_s, rr_r, at(a_, b_)))
    rrow[me] = drow[me]
    hop(2, d1p.at[1], r1m.at[1], at(a, bp))
    hop(3, d1m.at[0], r1p.at[0], at(a, bm))
    landed(rl1.at[0], 0)
    d1p[0] = (uf[0] + rl1[0].astype(F32)).astype(BF16)
    hop(4, d1p.at[0], r1m.at[0], at(a, bp))
    landed(rl1.at[1], 1)
    d1m[1] = (uf[1] + rl1[1].astype(F32)).astype(BF16)
    hop(5, d1m.at[1], r1p.at[1], at(a, bm))
    shares(b, 0, put_in(v1, 0))
    shares(b, 1, put_in(v1, 1))
    arrive(rrow.at[0:15], rr_r, rr_s)
    acc = rrow[0]
    for s in range(1, 16):
        acc = acc + rrow[s]
    zrow[...] = acc

    @pl.loop(0, 15)
    def _(k):
        zk = lax.rem(z + lax.rem(k + 4, 15) + 1, 16)
        push(zrow.at[zk], zbuf.at[z], z_s, z_r, (dp, zk))

    zbuf[z] = zrow[z]

    landed(r1m.at[1], 2)
    landed(r1p.at[0], 3)
    landed(r1m.at[0], 4)
    landed(r1p.at[1], 5)
    for h in range(2):
        v1[h] = v1[h] + r1m[h].astype(F32) + r1p[h].astype(F32)
        t2[h] = v1[h, a2].astype(BF16)
        if h == 0:
            hop(6, t2.at[0], rl2.at[0], at(ap, b))
            d2m[0] = v1[0, am].astype(BF16)
            hop(7, d2m.at[0], r2p.at[0], at(am, b))
        else:
            hop(8, t2.at[1], rl2.at[1], at(am, b))
            d2p[1] = v1[1, ap].astype(BF16)
            hop(9, d2p.at[1], r2m.at[1], at(ap, b))
    arrive(zbuf.at[0:15], z_r, z_s)
    acc = zbuf[0]
    for s in range(1, 16):
        acc = acc + zbuf[s]
    orow[...] = acc
    oall[core * 16 + me] = acc

    def back_to_all(a_, b_, s):
        row = core * 16 + me
        push(orow, oall.at[row], o_s, o_r, at(a_, b_))
        push(orow, oall.at[row], o_s, o_r, (a_ * sa + b_ * sb + other, z))

    peers(back_to_all)
    push(orow, oall.at[core * 16 + me], o_s, o_r, partner)

    landed(rl2.at[0], 6)
    d2p[0] = (v1[0, ap] + rl2[0].astype(F32)).astype(BF16)
    hop(10, d2p.at[0], r2m.at[0], at(ap, b))
    landed(rl2.at[1], 8)
    d2m[1] = (v1[1, am] + rl2[1].astype(F32)).astype(BF16)
    hop(11, d2m.at[1], r2p.at[1], at(am, b))
    landed(r2p.at[0], 7)
    landed(r2m.at[1], 9)
    landed(r2m.at[0], 10)
    landed(r2p.at[1], 11)
    qu = jnp.concatenate(
        [v1[h, a] + r2m[h].astype(F32) + r2p[h].astype(F32) for h in range(2)], axis=1
    )
    qv = q_ref[...].astype(F32)
    q_inv = 1.0 / jnp.sqrt(lanes_sum(qv * qv) + EPSILON)
    q_in = lanes_sum(qv * qu) * q_inv * q_inv
    gq_ref[...] = ((qu - qv * q_in) * q_inv).astype(BF16)
    gq_out = pltpu.make_async_copy(gq_ref, gq_hbm, out_s.at[1])
    gq_out.start()

    for c in rs + [p_copy, d_copy, w_copy, ab_copy]:
        c.wait_send()
    gone(qown.at[0:15], ag_s.at[0], q_r.at[0, 0])
    gone(qown, ag_s.at[1], qo_r)
    gone(ab.at[kind, 0 : 15 * 256], ab_s, ab_r)
    gone(csnd.at[0:15], c_s, c_r)
    gone(srcv.at[0:15], s_s, s_r)
    gone(grcv.at[0:15], g_s, g_r)
    gone(yrcv.at[0:15], y_s, y_r)
    gone(drow.at[0:15], rr_s, rr_r)
    gone(zrow.at[0:15], z_s, z_r)
    gone(oall.at[0:31], o_s, o_r)
    arrive(oall.at[0:31], o_r, o_s)
    outs = [gp_out, gq_out]
    for c_, dst in ((0, down_hbm), (1, up_hbm)):
        dv[c_, :, 0:128] = oall[c_ * 16 : c_ * 16 + 16, 0, :]
        dv[c_, :, 128:256] = oall[c_ * 16 : c_ * 16 + 16, 1, :]
        outs.append(pltpu.make_async_copy(dv.at[c_], dst, out_s.at[2 + c_]))
        outs[-1].start()

    for c in outs:
        c.wait()


def hand_over(*refs):
    copies = [pltpu.make_async_copy(refs[i], refs[4 + i], refs[8].at[i]) for i in (1, 0, 2, 3)]
    for c in copies:
        c.start()
    for c in copies:
        c.wait()


ANY = pl.BlockSpec(memory_space=pl.ANY)


def per_device(query, passage, query_attn, passage_attn, positives, negatives, home, down, up):
    dma = pltpu.SemaphoreType.DMA
    vm = pltpu.VMEM
    half = vm((2, 4, 16, H), BF16)
    row = vm((2, 16, H), BF16)
    grad_q, grad_p, sum_down, sum_up = pl.pallas_call(
        kernel,
        out_shape=(
            jax.ShapeDtypeStruct((16, D), BF16),
            jax.ShapeDtypeStruct((128, D), BF16),
            jax.ShapeDtypeStruct((16, 256), F32),
            jax.ShapeDtypeStruct((16, 256), F32),
        ),
        in_specs=[pl.BlockSpec(memory_space=pltpu.HBM)] * 9,
        out_specs=(ANY,) * 4,
        scratch_shapes=[
            vm((16, D), BF16),
            vm((128, D), BF16),
            vm((16, D), BF16),
            vm((128, D), BF16),
            vm((16, 64), I32),
            vm((32, 128), I32),
            vm((16, 256), BF16),
            vm((16, 256), BF16),
            pltpu.SMEM((1, 16), I32),
            vm((16, D), BF16),
            vm((128, D), BF16),
            vm((2, 16, 256), F32),
            vm((16, 2, 16, H), BF16),
            vm((16, 2, 16, H), BF16),
            vm((256, D), BF16),
            vm((32, D), BF16),
            vm((16, 128), I32),
            vm((256, H), BF16),
            vm((256, H), BF16),
            vm((16, 2, 16, 128), BF16),
            vm((16, 2, 16, 128), BF16),
            vm((4, 256, 64), F32),
            vm((4, 256, 64), F32),
            vm((2, 4, 128), F32),
            vm((16, 2, 4, 128), F32),
            vm((2, 4, 128), F32),
            vm((2, 256, 256), BF16),
            vm((2, 128, 256), BF16),
            vm((2, 256, 256), BF16),
            vm((16, 128), BF16),
            vm((16, 16, 128), BF16),
            vm((4, 16, 128), F32),
            vm((16, 16, 128), F32),
            half,
            half,
            half,
            half,
            half,
            half,
            vm((2, 4, 16, H), F32),
            vm((2, 4, 16, H), F32),
            row,
            row,
            row,
            row,
            row,
            row,
            vm((128, 128), F32),
            vm((128, D), F32),
            vm((32, D), F32),
            vm((16, D), F32),
            vm((16, 16, 2, 128), F32),
            vm((16, 16, 2, 128), F32),
            vm((16, 2, 128), F32),
            vm((16, 2, 128), F32),
            vm((2, 128), F32),
            vm((32, 2, 128), F32),
            dma((9,)),
            dma((4,)),
            dma((2,)),
            dma((16, 2)),
            dma(()),
            dma(()),
            dma(()),
            dma(()),
            dma(()),
            dma(()),
            dma(()),
            pltpu.SemaphoreType.REGULAR((6,)),
            dma(()),
            dma(()),
            dma(()),
            dma(()),
            dma(()),
            dma(()),
            dma(()),
            dma(()),
            dma(()),
            dma(()),
            dma((12,)),
            dma((12,)),
            dma(()),
            dma(()),
            dma(()),
            dma(()),
            dma(()),
            dma(()),
            dma(()),
            dma(()),
        ],
        compiler_params=pltpu.CompilerParams(
            collective_id=0, has_side_effects=True, vmem_limit_bytes=26 * 1024 * 1024
        ),
    )(
        *(
            pltpu.with_memory_space_constraint(v, pltpu.HBM)
            for v in (
                query[0], passage[0], query_attn[0], passage_attn[0], negatives[0],
                home[0].reshape(32, 128), down, up, positives,
            )
        )
    )
    outs = pl.pallas_call(
        hand_over,
        out_shape=tuple(jax.ShapeDtypeStruct(v.shape, v.dtype) for v in (grad_q, grad_p, sum_down, sum_up)),
        in_specs=[ANY] * 4,
        out_specs=(ANY,) * 4,
        scratch_shapes=[dma((4,))],
        compiler_params=pltpu.CompilerParams(vmem_limit_bytes=1024 * 1024),
    )(grad_q, grad_p, sum_down, sum_up)
    return outs[0][None], outs[1][None], outs[2], outs[3]


def solution(mesh):
    in_specs = (
        P("fsdp", "dp", None),
        P("fsdp", "dp", None),
        P("fsdp", "dp", None),
        P("fsdp", "dp", None),
        P("fsdp", "dp"),
        P("fsdp", "dp", None),
        P("fsdp", None),
        P(None, "fsdp"),
        P(None, "fsdp"),
    )
    out_specs = (P("fsdp", "dp", None), P("fsdp", "dp", None), P(None, "fsdp"), P(None, "fsdp"))
    return jax.shard_map(
        per_device, mesh=mesh, in_specs=in_specs, out_specs=out_specs, check_vma=False
    )
```
